128 devices in a mesh: gx: 4 (over y), gy: 8 (over z, core), sa: 4 (over x).
Axes of the slice: x: 4, y: 4, z: 4, core: 2. Of those that a mesh axis runs over, the one named last changes fastest.
Arguments:
- pixels: bfloat16 [16, 2048, 8192], P('sa', 'gy', 'gx'), may hold values from -6 to 6
- peak_offsets: int32 [16, 2, 32, 128], P('sa', None, 'gy', 'gx'), may hold values from -2 to 2
- validity: int32 [16, 32, 128], P('sa', 'gy', 'gx'), may hold values 0 or 1
Outputs:
- flow_field: float32 [16, 2, 32, 128], P('sa', None, 'gy', 'gx')
- mesh_field: float32 [16, 2, 32, 128], P('sa', None, 'gy', 'gx')
The draws below stay inside these ranges and needn't reach their ends.
All inputs are finite; a program needn't handle non-finite values. No bound on the sum of `validity` on one device may be relied on, other than what follows from the above.
Results may differ from the reference program's by a relative error of at most 0.0035.
Values may be sent and summed in bfloat16 or wider, within the bound.
No kernel may reach another device: no remote copies, remote signals or barrier semaphores. Data moves between devices by JAX's collectives and lax.ppermute only.
A program may use at most 192 MiB of HBM per device.

```python
import math
import jax
import jax.numpy as jnp
from jax import lax

PATCH = 64
RELAX = 8
SECTIONS = 16
ROWS = 2048
COLS = 8192
NR = 32
NC = 128


def plant(array, rng, smallest, high):
    index_at = [jax.random.randint(jax.random.fold_in(rng, axis), (), 0, length) for axis, length in enumerate(array.shape)]
    main_axis = array.shape.index(max(array.shape))
    next_to = index_at[:main_axis] + [(index_at[main_axis] + 1) % array.shape[main_axis]] + index_at[main_axis + 1:]
    return array.at[tuple(index_at)].set(smallest).at[tuple(next_to)].set(high)


def steps_of(stream_key, shape, pieces, least, largest):
    loudness, own = 1.0, jax.random.fold_in(stream_key, 6)
    for axis_at, blocks in pieces:
        draws = jnp.exp(jax.random.uniform(jax.random.fold_in(own, axis_at), (blocks,), jnp.float32, least / len(pieces), largest / len(pieces)))
        loudness = loudness * jnp.repeat(draws, shape[axis_at] // blocks).reshape([-1 if axis == axis_at else 1 for axis in range(len(shape))])
    return loudness


def gaussian(stream_key, extent, width, reach, pieces=(), kind=jnp.bfloat16):
    result = width * jax.random.normal(stream_key, extent, jnp.float32)
    if pieces:
        result = result * steps_of(stream_key, extent, pieces, -0.22, 0.18)
    return jnp.clip(result, -reach, reach).astype(kind)


def setup_inputs(seed: int = 0) -> dict:
    splits = jax.random.split(jax.random.key(seed), 4)
    pixels = gaussian(splits[0], (SECTIONS, ROWS, COLS), 1.0, 6.0, ((0, 4), (1, 8), (2, 4)))
    peak_offsets = plant(jax.random.randint(splits[1], (SECTIONS, 2, NR, NC), -2, 3), jax.random.fold_in(splits[1], 1), -2, 2).astype(jnp.int32)
    validity = plant((jax.random.randint(splits[2], (SECTIONS, NR, NC), 0, 4) < 3).astype(jnp.int32), jax.random.fold_in(splits[2], 1), 0, 1)
    return dict(pixels=pixels, peak_offsets=peak_offsets, validity=validity)


spring_plane = 0.5
spring_stack = 1.0
step_size = 0.2
damping = 0.6
whiten_floor = 1024.0

def to_half(values):
    return lax.optimization_barrier(values.astype(jnp.bfloat16)).astype(jnp.float32)

def dft_tables():
    frequency = jnp.arange(PATCH, dtype=jnp.int32)
    phases = frequency[:, None] * frequency[None, :] % PATCH
    angles = phases.astype(jnp.float32) * (2.0 * math.pi / PATCH)
    return (to_half(jnp.cos(angles)), to_half(jnp.sin(angles)))

def strip_spectrum(strip):
    cosine, sine_table = dft_tables()
    blocks = strip.astype(jnp.float32).reshape(PATCH, -1, PATCH)
    col_real = to_half(jnp.einsum('xbj,jk->xbk', blocks, cosine))
    col_imag = to_half(-jnp.einsum('xbj,jk->xbk', blocks, sine_table))
    spec_real = jnp.einsum('kx,xbj->kbj', cosine, col_real) + jnp.einsum('kx,xbj->kbj', sine_table, col_imag)
    spec_imag = jnp.einsum('kx,xbj->kbj', cosine, col_imag) - jnp.einsum('kx,xbj->kbj', sine_table, col_real)
    return (spec_real.astype(jnp.bfloat16), spec_imag.astype(jnp.bfloat16))

def phase_tables(offsets):
    frequency = jnp.arange(PATCH, dtype=jnp.int32)
    nearby = jnp.arange(3, dtype=jnp.int32) - 1
    phases = frequency[None, :, None] * (offsets[:, None, None] + nearby[None, None, :]) % PATCH
    angles = phases.astype(jnp.float32) * (2.0 * math.pi / PATCH)
    return (to_half(jnp.cos(angles)), to_half(jnp.sin(angles)))

def subpixel(correlation, offsets):
    center = correlation[..., 1, 1]
    row_low = correlation[..., 0, 1]
    row_high = correlation[..., 2, 1]
    col_low = correlation[..., 1, 0]
    col_high = correlation[..., 1, 2]
    row_step = (row_low - row_high) / (2.0 * jnp.maximum(jnp.abs(row_low - 2.0 * center + row_high), 1.0))
    col_step = (col_low - col_high) / (2.0 * jnp.maximum(jnp.abs(col_low - 2.0 * center + col_high), 1.0))
    return jnp.stack([offsets[0].astype(jnp.float32) + row_step, offsets[1].astype(jnp.float32) + col_step], 0)

def refine(current, previous, offsets):
    now_real = current[0].astype(jnp.float32)
    now_imag = current[1].astype(jnp.float32)
    old_real = previous[0].astype(jnp.float32)
    old_imag = previous[1].astype(jnp.float32)
    cross_real = now_real * old_real + now_imag * old_imag
    cross_imag = now_imag * old_real - now_real * old_imag
    scale = jnp.sqrt(cross_real * cross_real + cross_imag * cross_imag + whiten_floor * whiten_floor)
    prod_real = to_half(cross_real / scale)
    prod_imag = to_half(cross_imag / scale)
    col_cos, col_sin = phase_tables(offsets[1])
    row_cos, row_sin = phase_tables(offsets[0])
    high = lax.Precision.HIGHEST
    half_real = to_half(jnp.einsum('kbj,bjd->kbd', prod_real, col_cos, precision=high) - jnp.einsum('kbj,bjd->kbd', prod_imag, col_sin, precision=high))
    half_imag = to_half(jnp.einsum('kbj,bjd->kbd', prod_real, col_sin, precision=high) + jnp.einsum('kbj,bjd->kbd', prod_imag, col_cos, precision=high))
    correlation = (jnp.einsum('kbd,bke->bed', half_real, row_cos, precision=high) - jnp.einsum('kbd,bke->bed', half_imag, row_sin, precision=high)) / float(PATCH)
    return subpixel(correlation, offsets)

def relax(flow_field, validity):
    weight = validity.astype(jnp.float32)[:, None]
    mesh_state = jnp.cumsum(flow_field, axis=0)
    weight_next = jnp.concatenate([weight[1:], jnp.zeros_like(weight[:1])], 0)
    flow_next = jnp.concatenate([flow_field[1:], jnp.zeros_like(flow_field[:1])], 0)
    row_index = jnp.arange(NR, dtype=jnp.int32)[:, None]
    col_index = jnp.arange(NC, dtype=jnp.int32)[None, :]
    degree = 4.0 - (row_index == 0).astype(jnp.float32) - (row_index == NR - 1).astype(jnp.float32) - (col_index == 0).astype(jnp.float32) - (col_index == NC - 1).astype(jnp.float32)
    velocity = jnp.zeros_like(mesh_state)
    for iteration in range(RELAX):
        padded = jnp.pad(mesh_state, ((1, 1), (0, 0), (1, 1), (1, 1)))
        neighbours = padded[1:-1, :, :-2, 1:-1] + padded[1:-1, :, 2:, 1:-1] + padded[1:-1, :, 1:-1, :-2] + padded[1:-1, :, 1:-1, 2:]
        lower_mesh = padded[:-2, :, 1:-1, 1:-1]
        upper_mesh = padded[2:, :, 1:-1, 1:-1]
        here_term = weight * (mesh_state - lower_mesh - flow_field)
        next_term = weight_next * (upper_mesh - mesh_state - flow_next)
        gradient = spring_plane * (degree * mesh_state - neighbours) + spring_stack * (here_term - next_term)
        velocity = damping * velocity - step_size * gradient
        mesh_state = mesh_state + velocity
    return mesh_state

def reference(pixels, peak_offsets, validity):

    def one_section(section):
        section_image = lax.dynamic_index_in_dim(pixels, section, 0, keepdims=False)
        earlier_image = lax.dynamic_index_in_dim(pixels, jnp.maximum(section - 1, 0), 0, keepdims=False)
        earlier_image = jnp.where(section > 0, earlier_image, jnp.zeros_like(earlier_image))
        offsets = lax.dynamic_index_in_dim(peak_offsets, section, 0, keepdims=False)

        def one_strip(strip_index):
            start = (strip_index * PATCH).astype(jnp.int32)
            strip_now = lax.dynamic_slice_in_dim(section_image, start, PATCH, 0)
            strip_old = lax.dynamic_slice_in_dim(earlier_image, start, PATCH, 0)
            strip_offsets = lax.dynamic_index_in_dim(offsets, strip_index, 1, keepdims=False)
            return refine(strip_spectrum(strip_now), strip_spectrum(strip_old), strip_offsets)
        strips = lax.map(one_strip, jnp.arange(NR, dtype=jnp.int32))
        return jnp.transpose(strips, (1, 0, 2))
    flow_field = lax.map(one_section, jnp.arange(SECTIONS, dtype=jnp.int32))
    mesh_field = relax(flow_field, validity)
    return (flow_field, mesh_field)
```

```python
import functools
import math

import jax
import jax.numpy as jnp
import numpy as np
from jax import lax
from jax.experimental import pallas as pl
from jax.experimental.pallas import tpu as pltpu
from jax.sharding import PartitionSpec as P

PATCH = 64
RELAX = 8
HALF = PATCH // 2 + 1
PR = 4
KROWS = 144
LANES = 256
REACH = 3
SPAN = 2 * REACH + 1
AXES = ("gx", "gy", "sa")

spring_plane = 0.5
spring_stack = 1.0
step_size = 0.2
damping = 0.6
whiten_floor = 1024.0

BF = jnp.bfloat16
F32 = jnp.float32


def wave_tables():
    angles = np.arange(PATCH, dtype=np.float32) * np.float32(2.0 * math.pi / PATCH)
    cosine = np.cos(angles).astype(BF).astype(np.float32)
    sine = np.sin(angles).astype(BF).astype(np.float32)
    return cosine, sine


def row_matrix():
    cosine, sine = wave_tables()
    out = np.zeros((2, KROWS, PR * PATCH), np.float32)
    phase = np.arange(HALF)[:, None] * np.arange(PATCH)[None, :] % PATCH
    for pr in range(PR):
        rows = slice(pr * HALF, (pr + 1) * HALF)
        cols = slice(pr * PATCH, (pr + 1) * PATCH)
        out[0, rows, cols] = cosine[phase]
        out[1, rows, cols] = -sine[phase]
    return out.reshape(2 * KROWS, PR * PATCH).astype(BF)


def col_matrix():
    cosine, sine = wave_tables()
    phase = np.arange(PATCH)[:, None] * np.arange(PATCH)[None, :] % PATCH
    out = np.zeros((2, 2, PATCH, 2, 2, PATCH), np.float32)
    for p in range(2):
        out[0, p, :, 0, p] = cosine[phase]
        out[1, p, :, 0, p] = sine[phase]
        out[0, p, :, 1, p] = -sine[phase]
        out[1, p, :, 1, p] = cosine[phase]
    return out.reshape(256, 256).astype(BF)


def first_matrix(flip):
    cosine, sine = wave_tables()
    out = np.zeros((2, 32, 2, KROWS), np.float32)
    k1 = np.arange(HALF)
    weight = np.where((k1 == 0) | (k1 == PATCH // 2), 1.0, 2.0)
    for p1 in range(SPAN):
        phase = k1 * (p1 - REACH) % PATCH
        for pr in range(PR):
            sign = -1.0 if flip and pr >= PR // 2 else 1.0
            row, cols = p1 * PR + pr, slice(pr * HALF, (pr + 1) * HALF)
            out[0, row, 0, cols] = weight * cosine[phase]
            out[0, row, 1, cols] = -sign * weight * sine[phase]
            out[1, row, 0, cols] = weight * sine[phase]
            out[1, row, 1, cols] = sign * weight * cosine[phase]
    return out.reshape(64, 2 * KROWS).astype(BF)


def second_matrix(blocks):
    cosine, sine = wave_tables()
    out = np.zeros((blocks, 2, 4, PATCH, 8, blocks, 4), np.float32)
    k2 = np.arange(PATCH)
    for p2 in range(SPAN):
        phase = k2 * (p2 - REACH) % PATCH
        for j in range(blocks):
            for p in range(4):
                out[j, 0, p, :, p2, j, p] = cosine[phase]
                out[j, 1, p, :, p2, j, p] = -sine[phase]
    return out.reshape(blocks, 512, 8 * blocks * 4).astype(BF)


def spectrum(strips, rows_ref, cols_ref):
    half = jnp.dot(rows_ref[...], strips, preferred_element_type=F32).astype(BF)
    out = []
    for b in range(LANES // 128):
        lanes = slice(b * 128, (b + 1) * 128)
        both = jnp.concatenate([half[:KROWS, lanes], half[KROWS:, lanes]], axis=1)
        spec = jnp.dot(both, cols_ref[...], preferred_element_type=F32)
        out.append((spec[:, :128], spec[:, 128:]))
    return out


def whiten(now, old):
    real, imag = [], []
    for (now_real, now_imag), (old_real, old_imag) in zip(now, old):
        cross_real = now_real * old_real + now_imag * old_imag
        cross_imag = now_imag * old_real - now_real * old_imag
        power = cross_real * cross_real + cross_imag * cross_imag
        inverse = lax.rsqrt(power + whiten_floor * whiten_floor)
        real.append((cross_real * inverse).astype(BF))
        imag.append((cross_imag * inverse).astype(BF))
    return jnp.concatenate(
        [jnp.concatenate(real, axis=1), jnp.concatenate(imag, axis=1)], axis=0
    )


def first_sum(table_ref, prod):
    both = jnp.dot(table_ref[...], prod, preferred_element_type=F32)
    return jnp.concatenate([both[:32], both[32:]], axis=1)


def inner_kernel(px_ref, rows_ref, cols_ref, first_ref, second_ref, corr_ref, mix_ref):
    count = px_ref.shape[0]
    old, sums, edge = None, [], None
    for s in range(count):
        now = spectrum(px_ref[s], rows_ref, cols_ref)
        if s == 0:
            edge = now
        else:
            sums.append(first_sum(first_ref, whiten(now, old)).astype(BF))
        old = now
    low = lax.broadcasted_iota(jnp.int32, (KROWS, 128), 0) < 2 * HALF
    for b in range(LANES // 128):
        for part in range(2):
            mix_ref[part * KROWS : (part + 1) * KROWS, b * 128 : (b + 1) * 128] = jnp.where(
                low, edge[b][part], old[b][part]
            ).astype(BF)
    term = jnp.dot(jnp.concatenate(sums, axis=0), second_ref[0], preferred_element_type=F32)

    @pl.when(pl.program_id(0) == 0)
    def _():
        corr_ref[...] = term

    @pl.when(pl.program_id(0) > 0)
    def _():
        corr_ref[...] += term


def pick(pieces, offset):
    value = pieces[0]
    for i in range(1, 5):
        value = jnp.where(offset == i - 2, pieces[i], value)
    return value


def peak_step(low, center, high):
    bend = jnp.maximum(jnp.abs(low - 2.0 * center + high), 1.0)
    return (low - high) / (2.0 * bend)


def edge_kernel(
    up_ref, down_ref, extra_ref, mix_ref, rows_ref, cols_ref, first_ref, second_ref,
    inner_ref, offs_ref, valid_ref, flow_ref, load_ref, corr, picked, offs,
):
    sa = lax.axis_index("sa")
    step = pl.program_id(0)
    strips = jnp.concatenate([up_ref[...], down_ref[...]], axis=0)
    there = spectrum(strips, rows_ref, cols_ref)
    here = []
    for b in range(LANES // 128):
        lanes = slice(b * 128, (b + 1) * 128)
        here.append((mix_ref[:KROWS, lanes].astype(F32), mix_ref[KROWS:, lanes].astype(F32)))
    sums = first_sum(first_ref, whiten(here, there))
    pr = lax.broadcasted_iota(jnp.int32, sums.shape, 0) % PR
    dropped = ((sa == 0) & (pr < 2)) | ((sa == lax.axis_size("sa") - 1) & (pr >= 2))
    sums = jnp.where(dropped, 0.0, sums).astype(BF)
    term = jnp.dot(sums, second_ref[0], preferred_element_type=F32)

    @pl.when(step == 0)
    def _():
        corr[...] = term

    @pl.when(step > 0)
    def _():
        corr[...] += term

    @pl.when(step == pl.num_programs(0) - 1)
    def _():
        for p1 in range(SPAN):
            rows = slice(p1 * PR, (p1 + 1) * PR)
            picked[p1, 0:PR] = corr[rows]
            for s in range(3):
                picked[p1, (s + 1) * PR : (s + 2) * PR] = inner_ref[
                    s * 32 + p1 * PR : s * 32 + (p1 + 1) * PR
                ]
        extra = extra_ref[...].astype(F32).astype(jnp.int32)
        for c in range(2):
            for s in range(4):
                offs[c, s * PR : (s + 1) * PR, :] = offs_ref[s, c]
            offs[c, 2:4, :] = extra[c * 2 : c * 2 + 2, :32]
        row_off, col_off = offs[0], offs[1]
        wide = jnp.concatenate([row_off] * 8, axis=1)
        layers = [picked[p1] * (1.0 / PATCH) for p1 in range(SPAN)]
        low, mid, high = [pick(layers[d : d + 5], wide) for d in range(3)]

        def cut(layer, d):
            return pick([layer[:, (d + i) * 32 : (d + i + 1) * 32] for i in range(5)], col_off)

        center = cut(mid, 1)
        flows = (
            row_off.astype(F32) + peak_step(cut(low, 1), center, cut(high, 1)),
            col_off.astype(F32) + peak_step(cut(mid, 0), center, cut(mid, 2)),
        )
        load_ref[...] = jnp.zeros_like(load_ref)
        for s in range(4):
            lanes = slice(s * 32, (s + 1) * 32)
            for c in range(2):
                piece = flows[c][s * PR : (s + 1) * PR]
                flow_ref[c * PR : (c + 1) * PR, lanes] = piece
                load_ref[c * PR : (c + 1) * PR, lanes] = piece
            load_ref[2 * PR : 3 * PR, lanes] = valid_ref[s].astype(F32)


def relax_kernel(got_ref, own_ref, flow_out, mesh_out, raw, flow, coef, state, speed):
    gx, gy, sa = [lax.axis_index(a) for a in AXES]
    nx, ny, ns = [lax.axis_size(a) for a in AXES]
    lane = lax.broadcasted_iota(jnp.int32, (24, 128), 1)
    row = lax.broadcasted_iota(jnp.int32, (24, 128), 0)
    col = lane % 32
    raw[...] = jnp.zeros_like(raw)
    near = lax.broadcasted_iota(jnp.int32, (16, 128), 1) % 32 < 16
    left, right = jnp.maximum(gx - 1, 0), jnp.minimum(gx + 1, nx - 1)
    for g in range(5):
        gyc = jnp.clip(gy + g - 2, 0, ny - 1)
        for k in range(ns):
            mid = got_ref[(gx * ny + gyc) * ns + k].astype(F32)
            low = got_ref[(left * ny + gyc) * ns + k].astype(F32)
            high = got_ref[(right * ny + gyc) * ns + k].astype(F32)
            side = jnp.where(near, high, low)
            for c in range(3):
                raw[c, 0, k, g * PR : (g + 1) * PR, :] = mid[c * PR : (c + 1) * PR]
                raw[c, 1, k, g * PR : (g + 1) * PR, :] = side[c * PR : (c + 1) * PR]

    place = gy * PR - 2 * PR + row
    rows_ok = (place >= 0) & (place < ny * PR) & (row < 5 * PR)
    inside, degree = [], []
    for h in range(2):
        if h == 0:
            column = gx * 32 + col
        else:
            column = jnp.where(col < 16, (gx + 1) * 32 + col, (gx - 1) * 32 + col)
        ok = rows_ok & (column >= 0) & (column < nx * 32)
        inside.append(jnp.where(ok, 1.0, 0.0))
        edges = jnp.where(place == 0, 1.0, 0.0) + jnp.where(place == ny * PR - 1, 1.0, 0.0)
        edges += jnp.where(column == 0, 1.0, 0.0) + jnp.where(column == nx * 32 - 1, 1.0, 0.0)
        degree.append(4.0 - edges)

    swapped = (row % PR >= 2) & (lane < 32)
    for c in range(2):
        for h in range(2):
            carry = jnp.zeros((24, 128), F32)
            for k in range(ns):
                f = jnp.where(swapped, raw[c, h, (k + ns - 1) % ns], raw[c, h, k]) * inside[h]
                flow[c, h, k] = f
                x = f + jnp.where(lane >= 32, pltpu.roll(f, 32, 1), 0.0)
                x = x + jnp.where(lane >= 64, pltpu.roll(x, 64, 1), 0.0)
                state[0, c, h, k] = x + carry
                last = jnp.where(lane >= 96, x, 0.0)
                last = last + pltpu.roll(last, 64, 1)
                carry = carry + last + pltpu.roll(last, 32, 1)
                speed[c, h, k] = jnp.zeros((24, 128), F32)

    def above(get, k):
        up = get(k + 1) if k + 1 < ns else jnp.zeros((24, 128), F32)
        return pltpu.roll(jnp.where(lane < 32, up, get(k)), 96, 1)

    def below(get, k):
        down = get(k - 1) if k > 0 else jnp.zeros((24, 128), F32)
        return pltpu.roll(jnp.where(lane >= 96, down, get(k)), 32, 1)

    for h in range(2):
        for k in range(ns):
            w = raw[2, h, k] * inside[h] * (step_size * spring_stack)
            w_next = above(lambda i: raw[2, h, i], k) * inside[h] * (step_size * spring_stack)
            coef[0, h, k] = w
            coef[1, h, k] = w_next
            coef[2, h, k] = degree[h] * inside[h] * (step_size * spring_plane) + w + w_next
            for c in range(2):
                coef[3 + c, h, k] = w * flow[c, h, k] - w_next * above(lambda i: flow[c, h, i], k)

    plane = [inside[h] * (step_size * spring_plane) for h in range(2)]

    def advance(src, dst):
        for c in range(2):
            for h in range(2):
                for k in range(ns):
                    m, o = state[src, c, h, k], state[src, c, 1 - h, k]
                    get = lambda i: state[src, c, h, i]
                    around = jnp.where(col == 0, pltpu.roll(o, 97, 1), pltpu.roll(m, 1, 1))
                    around += jnp.where(col == 31, pltpu.roll(o, 31, 1), pltpu.roll(m, 127, 1))
                    around += pltpu.roll(m, 1, 0) + pltpu.roll(m, 23, 0)
                    v = damping * speed[c, h, k] - coef[2, h, k] * m + plane[h] * around
                    v += coef[0, h, k] * below(get, k) + coef[1, h, k] * above(get, k)
                    v += coef[3 + c, h, k]
                    speed[c, h, k] = v
                    state[dst, c, h, k] = m + v

    def two(i, unused):
        advance(0, 1)
        advance(1, 0)
        return unused

    lax.fori_loop(0, RELAX // 2, two, 0)
    mine = slice(2 * PR, 3 * PR)
    first = (lax.broadcasted_iota(jnp.int32, (PR, 128), 0) >= 2) & (
        lax.broadcasted_iota(jnp.int32, (PR, 128), 1) < 32
    )
    for c in range(2):
        m = state[0, c, 0, sa][mine]
        f = flow[c, 0, sa][mine]
        f = jnp.where(first, f, own_ref[c * PR : (c + 1) * PR])
        for s in range(4):
            lanes = slice(s * 32, (s + 1) * 32)
            mesh_out[s, c] = m[:, lanes]
            flow_out[s, c] = f[:, lanes]


def per_device(pixels, peak_offsets, validity):
    count, height, breadth = pixels.shape
    blocks = breadth // LANES
    size = lax.axis_size("sa")
    half = height // 2
    extra = peak_offsets[0, :, 2:, :].reshape(4, 32).astype(BF)
    extra = jnp.pad(extra, ((0, 12), (0, breadth - 32)))
    down = jnp.concatenate([pixels[0, half:], extra], axis=0)
    up = pixels[count - 1, :half]
    up = lax.ppermute(up, "sa", [(i, (i + 1) % size) for i in range(size)])
    down = lax.ppermute(down, "sa", [(i, (i - 1) % size) for i in range(size)])

    rows = jnp.asarray(row_matrix())
    cols = jnp.asarray(col_matrix())
    second = jnp.asarray(second_matrix(blocks))
    whole = lambda shape: pl.BlockSpec(shape, lambda j: (0,) * len(shape))
    table_specs = [
        whole((2 * KROWS, PR * PATCH)),
        whole((256, 256)),
        whole((64, 2 * KROWS)),
        pl.BlockSpec((1, 512, 8 * blocks * 4), lambda j: (j, 0, 0)),
    ]
    inner, mix = pl.pallas_call(
        inner_kernel,
        grid=(blocks,),
        in_specs=[pl.BlockSpec((count, height, LANES), lambda j: (0, 0, j))] + table_specs,
        out_specs=[
            whole((96, 256)),
            pl.BlockSpec((2 * KROWS, LANES), lambda j: (0, j)),
        ],
        out_shape=[
            jax.ShapeDtypeStruct((96, 256), F32),
            jax.ShapeDtypeStruct((2 * KROWS, breadth), BF),
        ],
        compiler_params=pltpu.CompilerParams(dimension_semantics=("arbitrary",)),
        cost_estimate=pl.CostEstimate(
            flops=8 * 10**9, bytes_accessed=8 * 2**20, transcendentals=10**6
        ),
        name="inner",
    )(pixels, rows, cols, jnp.asarray(first_matrix(False)), second)

    own, load = pl.pallas_call(
        edge_kernel,
        grid=(blocks,),
        in_specs=[
            pl.BlockSpec((half, LANES), lambda j: (0, j)),
            pl.BlockSpec((half, LANES), lambda j: (0, j)),
            pl.BlockSpec((16, 128), lambda j: (half // 16, 0)),
            pl.BlockSpec((2 * KROWS, LANES), lambda j: (0, j)),
        ]
        + table_specs
        + [whole((96, 256)), whole((count, 2, PR, 32)), whole((count, PR, 32))],
        out_specs=[whole((8, 128)), whole((16, 128))],
        out_shape=[
            jax.ShapeDtypeStruct((8, 128), F32),
            jax.ShapeDtypeStruct((16, 128), F32),
        ],
        scratch_shapes=[
            pltpu.VMEM((32, 256), F32),
            pltpu.VMEM((SPAN, 16, 256), F32),
            pltpu.VMEM((2, 16, 32), jnp.int32),
        ],
        compiler_params=pltpu.CompilerParams(dimension_semantics=("arbitrary",)),
        name="edge",
    )(
        up, down, down, mix, rows, cols, jnp.asarray(first_matrix(True)), second,
        inner, peak_offsets, validity,
    )

    devices = lax.axis_size(AXES)
    sent = jnp.broadcast_to(load.astype(BF)[None], (devices, 16, 128))
    got = lax.all_to_all(sent, AXES, 0, 0)

    field = (count, 2, PR, 32)
    vmem = lambda: pl.BlockSpec(memory_space=pltpu.VMEM)
    stack = (2, size, 24, 128)
    return pl.pallas_call(
        relax_kernel,
        in_specs=[vmem(), vmem()],
        out_specs=[vmem(), vmem()],
        out_shape=[jax.ShapeDtypeStruct(field, F32)] * 2,
        scratch_shapes=[
            pltpu.VMEM((3,) + stack, F32),
            pltpu.VMEM((2,) + stack, F32),
            pltpu.VMEM((5,) + stack, F32),
            pltpu.VMEM((2, 2) + stack, F32),
            pltpu.VMEM((2,) + stack, F32),
        ],
        name="relax",
    )(got, own)


def solution(mesh):
    return jax.shard_map(
        per_device,
        mesh=mesh,
        in_specs=(P("sa", "gy", "gx"), P("sa", None, "gy", "gx"), P("sa", "gy", "gx")),
        out_specs=(P("sa", None, "gy", "gx"), P("sa", None, "gy", "gx")),
        check_vma=False,
    )
```

```python
import math

import jax
import jax.numpy as jnp
import numpy as np
from jax import lax
from jax.experimental import pallas as pl
from jax.experimental.pallas import tpu as pltpu
from jax.sharding import PartitionSpec as P


PATCH = 64
RELAX = 8
HALF = PATCH // 2 + 1
PR = 4
KROWS = 144
LANES = 256
REACH = 3
SPAN = 2 * REACH + 1
GRANT = 20 * 2**20
AXES = ("gx", "gy", "sa")

spring_plane = 0.5
spring_stack = 1.0
step_size = 0.2
damping = 0.6
whiten_floor = 1024.0

BF = jnp.bfloat16
F32 = jnp.float32


def wave_tables():
    angles = np.arange(PATCH, dtype=np.float32) * np.float32(2.0 * math.pi / PATCH)
    cosine = np.cos(angles).astype(BF).astype(np.float32)
    sine = np.sin(angles).astype(BF).astype(np.float32)
    return cosine, sine


def row_matrix():
    cosine, sine = wave_tables()
    out = np.zeros((2, KROWS, PR * PATCH), np.float32)
    phase = np.arange(HALF)[:, None] * np.arange(PATCH)[None, :] % PATCH
    for pr in range(PR):
        rows = slice(pr * HALF, (pr + 1) * HALF)
        cols = slice(pr * PATCH, (pr + 1) * PATCH)
        out[0, rows, cols] = cosine[phase]
        out[1, rows, cols] = -sine[phase]
    return out.reshape(2 * KROWS, PR * PATCH).astype(BF)


def col_matrix():
    cosine, sine = wave_tables()
    phase = np.arange(PATCH)[:, None] * np.arange(PATCH)[None, :] % PATCH
    out = np.zeros((2, 2, PATCH, 2, 2, PATCH), np.float32)
    for p in range(2):
        out[0, p, :, 0, p] = cosine[phase]
        out[1, p, :, 0, p] = sine[phase]
        out[0, p, :, 1, p] = -sine[phase]
        out[1, p, :, 1, p] = cosine[phase]
    return out.reshape(256, 256).astype(BF)


def first_matrix(flip):
    cosine, sine = wave_tables()
    out = np.zeros((2, 32, 2, KROWS), np.float32)
    k1 = np.arange(HALF)
    weight = np.where((k1 == 0) | (k1 == PATCH // 2), 1.0, 2.0)
    for p1 in range(SPAN):
        phase = k1 * (p1 - REACH) % PATCH
        for pr in range(PR):
            sign = -1.0 if flip and pr >= PR // 2 else 1.0
            row, cols = p1 * PR + pr, slice(pr * HALF, (pr + 1) * HALF)
            out[0, row, 0, cols] = weight * cosine[phase]
            out[0, row, 1, cols] = -sign * weight * sine[phase]
            out[1, row, 0, cols] = weight * sine[phase]
            out[1, row, 1, cols] = sign * weight * cosine[phase]
    return out.reshape(64, 2 * KROWS).astype(BF)


def second_matrix(blocks):
    cosine, sine = wave_tables()
    out = np.zeros((blocks, 2, 4, PATCH, 8, blocks, 4), np.float32)
    k2 = np.arange(PATCH)
    for p2 in range(SPAN):
        phase = k2 * (p2 - REACH) % PATCH
        for j in range(blocks):
            for p in range(4):
                out[j, 0, p, :, p2, j, p] = cosine[phase]
                out[j, 1, p, :, p2, j, p] = -sine[phase]
    return out.reshape(blocks, 512, 8 * blocks * 4).astype(BF)


def whiten(now, old):
    real, imag = [], []
    for (now_real, now_imag), (old_real, old_imag) in zip(now, old):
        cross_real = now_real * old_real + now_imag * old_imag
        cross_imag = now_imag * old_real - now_real * old_imag
        power = cross_real * cross_real + cross_imag * cross_imag
        inverse = lax.rsqrt(power + whiten_floor * whiten_floor)
        real.append((cross_real * inverse).astype(BF))
        imag.append((cross_imag * inverse).astype(BF))
    return jnp.concatenate(
        [jnp.concatenate(real, axis=1), jnp.concatenate(imag, axis=1)], axis=0
    )


def first_sum(table_ref, prod):
    both = jnp.dot(table_ref[...], prod, preferred_element_type=F32)
    return jnp.concatenate([both[:32], both[32:]], axis=1)


def send_kernel(px_ref, offs_ref, up_ref, down_ref, offs, low, sems, offs_sem):
    count, height, breadth = px_ref.shape
    half = height // 2
    copies = []
    for b in range(breadth // 128):
        rows, lanes = pl.ds(b * half, half), pl.ds(b * 128, 128)
        copies += [
            pltpu.make_async_copy(
                px_ref.at[count - 1, pl.ds(0, half), lanes], up_ref.at[rows], sems.at[0, b]
            ),
            pltpu.make_async_copy(
                px_ref.at[0, pl.ds(half, half), lanes], down_ref.at[rows], sems.at[1, b]
            ),
        ]
    first = pltpu.make_async_copy(offs_ref.at[0], offs, offs_sem)
    first.start()
    for copy in copies:
        copy.start()
    low[...] = jnp.zeros_like(low)
    first.wait()
    for c in range(2):
        low[c * 2 : c * 2 + 2, :32] = offs[c, 2:4].astype(F32)
    down_ref[breadth * half // 128 :, :] = low[...].astype(BF)
    for copy in copies:
        copy.wait()


def row_sum(strips, rows_ref):
    return jnp.dot(rows_ref[...], strips, preferred_element_type=F32).astype(BF)


def col_sum(half, cols_ref):
    out = []
    for b in range(LANES // 128):
        lanes = slice(b * 128, (b + 1) * 128)
        both = jnp.concatenate([half[:KROWS, lanes], half[KROWS:, lanes]], axis=1)
        spec = jnp.dot(both, cols_ref[...], preferred_element_type=F32)
        out.append((spec[:, :128], spec[:, 128:]))
    return out


def inner_kernel(px_ref, rows_ref, cols_ref, first_ref, second_ref, corr_ref, mix_ref):
    count = px_ref.shape[0]
    sums, specs = [], []
    half = row_sum(px_ref[0], rows_ref)
    prod = None
    for s in range(count):
        specs.append(col_sum(half, cols_ref))
        if s + 1 < count:
            half = row_sum(px_ref[s + 1], rows_ref)
        if prod is not None:
            sums.append(first_sum(first_ref, prod).astype(BF))
        prod = whiten(specs[s], specs[s - 1]) if s else None
    sums.append(first_sum(first_ref, prod).astype(BF))
    edge, old = specs[0], specs[-1]
    low = lax.broadcasted_iota(jnp.int32, (KROWS, 128), 0) < 2 * HALF
    for b in range(LANES // 128):
        for part in range(2):
            mix_ref[part * KROWS : (part + 1) * KROWS, b * 128 : (b + 1) * 128] = jnp.where(
                low, edge[b][part], old[b][part]
            ).astype(BF)
    term = jnp.dot(jnp.concatenate(sums, axis=0), second_ref[0], preferred_element_type=F32)

    @pl.when(pl.program_id(0) == 0)
    def _():
        corr_ref[...] = term

    @pl.when(pl.program_id(0) > 0)
    def _():
        corr_ref[...] += term


def pick(pieces, offset):
    value = pieces[0]
    for i in range(1, 5):
        value = jnp.where(offset == i - 2, pieces[i], value)
    return value


def peak_step(low, center, high):
    bend = jnp.maximum(jnp.abs(low - 2.0 * center + high), 1.0)
    return (low - high) / (2.0 * bend)


def edge_kernel(
    up_ref, down_ref, mix_ref, rows_ref, cols_ref, first_ref, second_ref,
    inner_ref, offs_ref, valid_ref, flow_ref, load_ref, picked, offs, packed,
):
    sa = lax.axis_index("sa")
    breadth = mix_ref.shape[1]
    half = up_ref.shape[0] * 128 // breadth
    pr = lax.broadcasted_iota(jnp.int32, (32, 512), 0) % PR
    dropped = ((sa == 0) & (pr < 2)) | ((sa == lax.axis_size("sa") - 1) & (pr >= 2))

    def strips(j):
        parts = []
        for b in range(2 * j, 2 * j + 2):
            rows = slice(b * half, (b + 1) * half)
            parts.append(jnp.concatenate([up_ref[rows], down_ref[rows]], axis=0))
        return jnp.concatenate(parts, axis=1)

    blocks = breadth // LANES
    corr = jnp.zeros((32, 256), F32)
    row = row_sum(strips(0), rows_ref)
    prod = None
    for j in range(blocks + 1):
        if j < blocks:
            there = col_sum(row, cols_ref)
            if j + 1 < blocks:
                row = row_sum(strips(j + 1), rows_ref)
        if j:
            sums = first_sum(first_ref, prod)
            sums = jnp.where(dropped, 0.0, sums).astype(BF)
            corr += jnp.dot(sums, second_ref[j - 1], preferred_element_type=F32)
        if j < blocks:
            here = []
            for b in range(2 * j, 2 * j + 2):
                part = slice(b * 128, (b + 1) * 128)
                here.append((mix_ref[:KROWS, part].astype(F32), mix_ref[KROWS:, part].astype(F32)))
            prod = whiten(here, there)

    for p1 in range(SPAN):
        picked[p1, 0:PR] = corr[p1 * PR : (p1 + 1) * PR]
        for s in range(3):
            picked[p1, (s + 1) * PR : (s + 2) * PR] = inner_ref[
                s * 32 + p1 * PR : s * 32 + (p1 + 1) * PR
            ]
    extra = down_ref[breadth * half // 128 :, :].astype(F32).astype(jnp.int32)
    for c in range(2):
        for s in range(4):
            offs[c, s * PR : (s + 1) * PR, :] = offs_ref[s, c]
        offs[c, 2:4, :] = extra[c * 2 : c * 2 + 2, :32]
    row_off, col_off = offs[0], offs[1]
    wide = jnp.concatenate([row_off] * 8, axis=1)
    layers = [picked[p1] * (1.0 / PATCH) for p1 in range(SPAN)]
    low, mid, high = [pick(layers[d : d + 5], wide) for d in range(3)]

    def cut(layer, d):
        return pick([layer[:, (d + i) * 32 : (d + i + 1) * 32] for i in range(5)], col_off)

    center = cut(mid, 1)
    flows = (
        row_off.astype(F32) + peak_step(cut(low, 1), center, cut(high, 1)),
        col_off.astype(F32) + peak_step(cut(mid, 0), center, cut(mid, 2)),
    )
    weights = jnp.concatenate([valid_ref[s].astype(F32) for s in range(4)], axis=0)
    for c, field in enumerate(flows + (weights,)):
        ring = jnp.concatenate([field[:, 16:], field, field[:, :16]], axis=1)
        for s in range(4):
            rows = slice(s * PR, (s + 1) * PR)
            if c < 2:
                flow_ref[c * PR : (c + 1) * PR, s * 32 : (s + 1) * 32] = field[rows]
            at = (s % 2) * 12 + c * PR
            packed[at : at + PR, (s // 2) * 64 : (s // 2 + 1) * 64] = ring[rows]
    load_ref[...] = packed[...].astype(BF)


def relax_kernel(got_ref, own_ref, flow_out, mesh_out, raw, flow, coef, state, speed):
    gx, gy, sa = [lax.axis_index(a) for a in AXES]
    nx, ny, ns = [lax.axis_size(a) for a in AXES]
    shape = (24, 128)
    lane = lax.broadcasted_iota(jnp.int32, shape, 1)
    row = lax.broadcasted_iota(jnp.int32, shape, 0)
    low = lane < 64
    for c in range(3):
        for i in range(2):
            for k in range(ns):
                raw[c, i, k, 20:, :] = jnp.zeros((4, 128), F32)
    for g in range(5):
        at = jnp.clip(gy + g - 2, 0, ny - 1) * ns
        for k in range(ns):
            block = got_ref[at + k].astype(F32)
            for i in range(2):
                for c in range(3):
                    raw[c, i, k, g * PR : (g + 1) * PR, :] = block[
                        i * 12 + c * PR : i * 12 + (c + 1) * PR
                    ]

    place = gy * PR - 2 * PR + row
    column = gx * 32 - 16 + lane % 64
    ok = (place >= 0) & (place < ny * PR) & (row < 5 * PR) & (column >= 0) & (column < nx * 32)
    inside = jnp.where(ok, 1.0, 0.0)
    edges = jnp.where(place == 0, 1.0, 0.0) + jnp.where(place == ny * PR - 1, 1.0, 0.0)
    edges += jnp.where(column == 0, 1.0, 0.0) + jnp.where(column == nx * 32 - 1, 1.0, 0.0)
    degree = 4.0 - edges
    zero = jnp.zeros(shape, F32)

    swapped = (row % PR >= 2) & low
    for c in range(2):
        carry = zero
        for k in range(ns):
            even = jnp.where(swapped, raw[c, 0, (k + ns - 1) % ns], raw[c, 0, k]) * inside
            odd = raw[c, 1, k] * inside
            flow[c, 0, k] = even
            flow[c, 1, k] = odd
            pair = even + odd
            turned = pltpu.roll(pair, 64, 1)
            even = even + jnp.where(low, 0.0, turned) + carry
            state[0, c, 0, k] = even
            state[0, c, 1, k] = even + odd
            carry = carry + pair + turned
            speed[c, 0, k] = zero
            speed[c, 1, k] = zero

    def below(get, i, k):
        if i == 1:
            return get(0, k)
        return pltpu.roll(jnp.where(low, get(1, k), get(1, k - 1) if k else 0.0), 64, 1)

    def above(get, i, k):
        if i == 0:
            return get(1, k)
        return pltpu.roll(jnp.where(low, get(0, k + 1) if k + 1 < ns else 0.0, get(0, k)), 64, 1)

    plane = inside * (step_size * spring_plane)
    stack = inside * (step_size * spring_stack)
    for i in range(2):
        for k in range(ns):
            w = raw[2, i, k] * stack
            w_next = above(lambda i, k: raw[2, i, k], i, k) * stack
            coef[0, i, k] = w
            coef[1, i, k] = w_next
            coef[2, i, k] = degree * plane + w + w_next
            for c in range(2):
                get = lambda i, k: flow[c, i, k]
                coef[3 + c, i, k] = w * get(i, k) - w_next * above(get, i, k)

    def advance(src, dst):
        for c in range(2):
            get = lambda i, k: state[src, c, i, k]
            for k in range(ns):
                for i in range(2):
                    m = get(i, k)
                    around = pltpu.roll(m, 1, 1) + pltpu.roll(m, 127, 1)
                    around += pltpu.roll(m, 1, 0) + pltpu.roll(m, 23, 0)
                    v = damping * speed[c, i, k] - coef[2, i, k] * m + plane * around
                    v += coef[0, i, k] * below(get, i, k) + coef[1, i, k] * above(get, i, k)
                    v += coef[3 + c, i, k]
                    speed[c, i, k] = v
                    state[dst, c, i, k] = m + v

    def two(step, unused):
        advance(0, 1)
        advance(1, 0)
        return unused

    lax.fori_loop(0, RELAX // 2, two, 0)
    mine = slice(2 * PR, 3 * PR)
    late = lax.broadcasted_iota(jnp.int32, (PR, 32), 0) >= 2
    for c in range(2):
        for s in range(4):
            lanes = slice((s // 2) * 64 + 16, (s // 2) * 64 + 48)
            mesh_out[s, c] = state[0, c, s % 2, sa][mine, lanes]
            f = own_ref[c * PR : (c + 1) * PR, s * 32 : (s + 1) * 32]
            if s == 0:
                f = jnp.where(late, flow[c, 0, sa][mine, lanes], f)
            flow_out[s, c] = f


def per_device(pixels, peak_offsets, validity):
    count, height, breadth = pixels.shape
    blocks = breadth // LANES
    size = lax.axis_size("sa")
    half = height // 2
    vmem = lambda: pl.BlockSpec(memory_space=pltpu.VMEM)
    held = pltpu.with_memory_space_constraint(pixels, pltpu.HBM)
    packed = breadth * half // 128
    up, down = pl.pallas_call(
        send_kernel,
        in_specs=[pl.BlockSpec(memory_space=pltpu.HBM)] * 2,
        out_specs=[vmem(), vmem()],
        out_shape=[
            jax.ShapeDtypeStruct((packed, 128), BF),
            jax.ShapeDtypeStruct((packed + 8, 128), BF),
        ],
        scratch_shapes=[
            pltpu.VMEM((2, PR, 32), jnp.int32),
            pltpu.VMEM((8, 128), F32),
            pltpu.SemaphoreType.DMA((2, breadth // 128)),
            pltpu.SemaphoreType.DMA,
        ],
        compiler_params=pltpu.CompilerParams(vmem_limit_bytes=GRANT),
        name="send",
    )(held, pltpu.with_memory_space_constraint(peak_offsets, pltpu.HBM))
    up = lax.ppermute(up, "sa", [(i, (i + 1) % size) for i in range(size)])
    down = lax.ppermute(down, "sa", [(i, (i - 1) % size) for i in range(size)])

    rows = jnp.asarray(row_matrix())
    cols = jnp.asarray(col_matrix())
    second = jnp.asarray(second_matrix(blocks))
    whole = lambda shape: pl.BlockSpec(shape, lambda j: (0,) * len(shape))
    table_specs = [
        whole((2 * KROWS, PR * PATCH)),
        whole((256, 256)),
        whole((64, 2 * KROWS)),
        pl.BlockSpec((1, 512, 8 * blocks * 4), lambda j: (j, 0, 0)),
    ]
    inner, mix = pl.pallas_call(
        inner_kernel,
        grid=(blocks,),
        in_specs=[pl.BlockSpec((count, height, LANES), lambda j: (0, 0, j))] + table_specs,
        out_specs=[
            whole((96, 256)),
            pl.BlockSpec((2 * KROWS, LANES), lambda j: (0, j)),
        ],
        out_shape=[
            jax.ShapeDtypeStruct((96, 256), F32),
            jax.ShapeDtypeStruct((2 * KROWS, breadth), BF),
        ],
        compiler_params=pltpu.CompilerParams(dimension_semantics=("arbitrary",), vmem_limit_bytes=GRANT),
        cost_estimate=pl.CostEstimate(
            flops=8 * 10**9, bytes_accessed=8 * 2**20, transcendentals=10**6
        ),
        name="inner",
    )(
        held, rows, cols, jnp.asarray(first_matrix(False)), second,
    )

    own, load = pl.pallas_call(
        edge_kernel,
        in_specs=[vmem()] * 10,
        out_specs=[vmem(), vmem()],
        out_shape=[
            jax.ShapeDtypeStruct((8, 128), F32),
            jax.ShapeDtypeStruct((24, 128), BF),
        ],
        scratch_shapes=[
            pltpu.VMEM((SPAN, 16, 256), F32),
            pltpu.VMEM((2, 16, 32), jnp.int32),
            pltpu.VMEM((24, 128), F32),
        ],
        compiler_params=pltpu.CompilerParams(vmem_limit_bytes=GRANT),
        name="edge",
    )(
        up, down, mix, rows, cols, jnp.asarray(first_matrix(True)), second,
        inner, peak_offsets, validity,
    )

    breadths = lax.axis_size("gx")
    near = lax.ppermute(load, "gx", [(i, i ^ 1) for i in range(breadths)])
    far = [(i, ((i + 1) ^ 1) - 1) for i in range(1, breadths - 1)]
    far = lax.ppermute(load, "gx", far)
    odd = lax.axis_index("gx") % 2 == 1
    place = lax.broadcasted_iota(jnp.int32, load.shape, 1) % 64
    side = jnp.where((place < 16) == odd, near, far)
    load = jnp.where((place >= 16) & (place < 48), load, side)
    devices = lax.axis_size(("gy", "sa"))
    sent = jnp.broadcast_to(load[None], (devices,) + load.shape)
    got = lax.all_to_all(sent, ("gy", "sa"), 0, 0)

    field = (count, 2, PR, 32)
    stack = (2, size, 24, 128)
    return pl.pallas_call(
        relax_kernel,
        in_specs=[vmem(), vmem()],
        out_specs=[vmem(), vmem()],
        out_shape=[jax.ShapeDtypeStruct(field, F32)] * 2,
        scratch_shapes=[
            pltpu.VMEM((3,) + stack, F32),
            pltpu.VMEM((2,) + stack, F32),
            pltpu.VMEM((5,) + stack, F32),
            pltpu.VMEM((2, 2) + stack, F32),
            pltpu.VMEM((2,) + stack, F32),
        ],
        compiler_params=pltpu.CompilerParams(vmem_limit_bytes=GRANT),
        name="relax",
    )(got, own)


def solution(mesh):
    return jax.shard_map(
        per_device,
        mesh=mesh,
        in_specs=(P("sa", "gy", "gx"), P("sa", None, "gy", "gx"), P("sa", "gy", "gx")),
        out_specs=(P("sa", None, "gy", "gx"), P("sa", None, "gy", "gx")),
        check_vma=False,
    )
```

```python
import math

import jax
import jax.numpy as jnp
import numpy as np
from jax import lax
from jax.experimental import pallas as pl
from jax.experimental.pallas import tpu as pltpu
from jax.sharding import PartitionSpec as P


PATCH = 64
RELAX = 8
HALF = PATCH // 2 + 1
PR = 4
KROWS = 144
LANES = 512
SUB = LANES // 128
HELD = LANES // PATCH
REACH = 3
SPAN = 2 * REACH + 1
GRANT = 20 * 2**20
AXES = ("gx", "gy", "sa")

spring_plane = 0.5
spring_stack = 1.0
step_size = 0.2
damping = 0.6
whiten_floor = 1024.0

BF = jnp.bfloat16
F32 = jnp.float32


def wave_tables():
    angles = np.arange(PATCH, dtype=np.float32) * np.float32(2.0 * math.pi / PATCH)
    cosine = np.cos(angles).astype(BF).astype(np.float32)
    sine = np.sin(angles).astype(BF).astype(np.float32)
    return cosine, sine


def row_matrix():
    cosine, sine = wave_tables()
    out = np.zeros((2, KROWS, PR * PATCH), np.float32)
    phase = np.arange(HALF)[:, None] * np.arange(PATCH)[None, :] % PATCH
    for pr in range(PR):
        rows = slice(pr * HALF, (pr + 1) * HALF)
        cols = slice(pr * PATCH, (pr + 1) * PATCH)
        out[0, rows, cols] = cosine[phase]
        out[1, rows, cols] = -sine[phase]
    return out.reshape(2 * KROWS, PR * PATCH).astype(BF)


def col_matrix():
    cosine, sine = wave_tables()
    phase = np.arange(PATCH)[:, None] * np.arange(PATCH)[None, :] % PATCH
    out = np.zeros((2, 2, PATCH, 2, 2, PATCH), np.float32)
    for p in range(2):
        out[0, p, :, 0, p] = cosine[phase]
        out[1, p, :, 0, p] = sine[phase]
        out[0, p, :, 1, p] = -sine[phase]
        out[1, p, :, 1, p] = cosine[phase]
    return out.reshape(256, 256).astype(BF)


def first_matrix(flip):
    cosine, sine = wave_tables()
    out = np.zeros((2, 32, 2, KROWS), np.float32)
    k1 = np.arange(HALF)
    weight = np.where((k1 == 0) | (k1 == PATCH // 2), 1.0, 2.0)
    for p1 in range(SPAN):
        phase = k1 * (p1 - REACH) % PATCH
        for pr in range(PR):
            sign = -1.0 if flip and pr >= PR // 2 else 1.0
            row, cols = p1 * PR + pr, slice(pr * HALF, (pr + 1) * HALF)
            out[0, row, 0, cols] = weight * cosine[phase]
            out[0, row, 1, cols] = -sign * weight * sine[phase]
            out[1, row, 0, cols] = weight * sine[phase]
            out[1, row, 1, cols] = sign * weight * cosine[phase]
    return out.reshape(64, 2 * KROWS).astype(BF)


def second_matrix(blocks):
    cosine, sine = wave_tables()
    out = np.zeros((blocks, 2, HELD, PATCH, 8, blocks, HELD), np.float32)
    k2 = np.arange(PATCH)
    for p2 in range(SPAN):
        phase = k2 * (p2 - REACH) % PATCH
        for j in range(blocks):
            for p in range(HELD):
                out[j, 0, p, :, p2, j, p] = cosine[phase]
                out[j, 1, p, :, p2, j, p] = -sine[phase]
    return out.reshape(blocks, 2 * LANES, 8 * blocks * HELD).astype(BF)


def whiten(now, old):
    real, imag = [], []
    for (now_real, now_imag), (old_real, old_imag) in zip(now, old):
        cross_real = now_real * old_real + now_imag * old_imag
        cross_imag = now_imag * old_real - now_real * old_imag
        power = cross_real * cross_real + cross_imag * cross_imag
        inverse = lax.rsqrt(power + whiten_floor * whiten_floor)
        real.append((cross_real * inverse).astype(BF))
        imag.append((cross_imag * inverse).astype(BF))
    return jnp.concatenate(
        [jnp.concatenate(real, axis=1), jnp.concatenate(imag, axis=1)], axis=0
    )


def first_sum(table_ref, prod):
    both = jnp.dot(table_ref[...], prod, preferred_element_type=F32)
    return jnp.concatenate([both[:32], both[32:]], axis=1)


def send_kernel(px_ref, offs_ref, up_ref, down_ref, extra_ref, offs, low, sems):
    half = up_ref.shape[0]
    last = px_ref.shape[0] - 1
    copies = [
        pltpu.make_async_copy(offs_ref.at[0], offs, sems.at[0]),
        pltpu.make_async_copy(px_ref.at[last, pl.ds(0, half)], up_ref, sems.at[1]),
        pltpu.make_async_copy(px_ref.at[0, pl.ds(half, half)], down_ref, sems.at[2]),
    ]
    for copy in copies:
        copy.start()
    low[...] = jnp.zeros_like(low)
    copies[0].wait()
    for c in range(2):
        low[c * 2 : c * 2 + 2, :32] = offs[c, 2:4].astype(F32)
    extra_ref[...] = low[...].astype(BF)
    for copy in copies[1:]:
        copy.wait()


def row_sum(strips, rows_ref):
    return jnp.dot(rows_ref[...], strips, preferred_element_type=F32).astype(BF)


def col_sum(half, cols_ref):
    both = []
    for b in range(SUB):
        lanes = slice(b * 128, (b + 1) * 128)
        both.append(jnp.concatenate([half[:KROWS, lanes], half[KROWS:, lanes]], axis=1))
    spec = jnp.dot(jnp.concatenate(both, axis=0), cols_ref[...], preferred_element_type=F32)
    out = []
    for b in range(SUB):
        rows = slice(b * KROWS, (b + 1) * KROWS)
        out.append((spec[rows, :128], spec[rows, 128:]))
    return out


def inner_kernel(px_ref, rows_ref, cols_ref, first_ref, second_ref, corr_ref, mix_ref):
    count = px_ref.shape[0]
    sums, specs = [], []
    half = row_sum(px_ref[0], rows_ref)
    prod = None
    for s in range(count):
        specs.append(col_sum(half, cols_ref))
        if s + 1 < count:
            half = row_sum(px_ref[s + 1], rows_ref)
        if prod is not None:
            sums.append(first_sum(first_ref, prod).astype(BF))
        prod = whiten(specs[s], specs[s - 1]) if s else None
    sums.append(first_sum(first_ref, prod).astype(BF))
    edge, old = specs[0], specs[-1]
    low = lax.broadcasted_iota(jnp.int32, (KROWS, 128), 0) < 2 * HALF
    for b in range(SUB):
        for part in range(2):
            mix_ref[part * KROWS : (part + 1) * KROWS, b * 128 : (b + 1) * 128] = jnp.where(
                low, edge[b][part], old[b][part]
            ).astype(BF)
    term = jnp.dot(jnp.concatenate(sums, axis=0), second_ref[0], preferred_element_type=F32)

    @pl.when(pl.program_id(0) == 0)
    def _():
        corr_ref[...] = term

    @pl.when(pl.program_id(0) > 0)
    def _():
        corr_ref[...] += term


def pick(pieces, offset):
    value = pieces[0]
    for i in range(1, 5):
        value = jnp.where(offset == i - 2, pieces[i], value)
    return value


def peak_step(low, center, high):
    bend = jnp.maximum(jnp.abs(low - 2.0 * center + high), 1.0)
    return (low - high) / (2.0 * bend)


def edge_kernel(
    up_ref, down_ref, extra_ref, mix_ref, rows_ref, cols_ref, first_ref, second_ref,
    inner_ref, offs_ref, valid_ref, flow_ref, load_ref, picked, offs, packed,
):
    sa = lax.axis_index("sa")
    breadth = mix_ref.shape[1]
    pr = lax.broadcasted_iota(jnp.int32, (32, 2 * LANES), 0) % PR
    dropped = ((sa == 0) & (pr < 2)) | ((sa == lax.axis_size("sa") - 1) & (pr >= 2))

    def strips(j):
        lanes = slice(j * LANES, (j + 1) * LANES)
        return jnp.concatenate([up_ref[:, lanes], down_ref[:, lanes]], axis=0)

    blocks = breadth // LANES
    corr = jnp.zeros((32, 256), F32)
    row = row_sum(strips(0), rows_ref)
    prod = None
    for j in range(blocks + 1):
        if j < blocks:
            there = col_sum(row, cols_ref)
            if j + 1 < blocks:
                row = row_sum(strips(j + 1), rows_ref)
        if j:
            sums = first_sum(first_ref, prod)
            sums = jnp.where(dropped, 0.0, sums).astype(BF)
            corr += jnp.dot(sums, second_ref[j - 1], preferred_element_type=F32)
        if j < blocks:
            here = []
            for b in range(SUB * j, SUB * (j + 1)):
                part = slice(b * 128, (b + 1) * 128)
                here.append((mix_ref[:KROWS, part].astype(F32), mix_ref[KROWS:, part].astype(F32)))
            prod = whiten(here, there)

    for p1 in range(SPAN):
        picked[p1, 0:PR] = corr[p1 * PR : (p1 + 1) * PR]
        for s in range(3):
            picked[p1, (s + 1) * PR : (s + 2) * PR] = inner_ref[
                s * 32 + p1 * PR : s * 32 + (p1 + 1) * PR
            ]
    extra = extra_ref[...].astype(F32).astype(jnp.int32)
    for c in range(2):
        for s in range(4):
            offs[c, s * PR : (s + 1) * PR, :] = offs_ref[s, c]
        offs[c, 2:4, :] = extra[c * 2 : c * 2 + 2, :32]
    row_off, col_off = offs[0], offs[1]
    wide = jnp.concatenate([row_off] * 8, axis=1)
    layers = [picked[p1] * (1.0 / PATCH) for p1 in range(SPAN)]
    low, mid, high = [pick(layers[d : d + 5], wide) for d in range(3)]

    def cut(layer, d):
        return pick([layer[:, (d + i) * 32 : (d + i + 1) * 32] for i in range(5)], col_off)

    center = cut(mid, 1)
    flows = (
        row_off.astype(F32) + peak_step(cut(low, 1), center, cut(high, 1)),
        col_off.astype(F32) + peak_step(cut(mid, 0), center, cut(mid, 2)),
    )
    weights = jnp.concatenate([valid_ref[s].astype(F32) for s in range(4)], axis=0)
    for c, field in enumerate(flows + (weights,)):
        ring = jnp.concatenate([field[:, 16:], field, field[:, :16]], axis=1)
        for s in range(4):
            rows = slice(s * PR, (s + 1) * PR)
            if c < 2:
                flow_ref[c * PR : (c + 1) * PR, s * 32 : (s + 1) * 32] = field[rows]
            at = (s % 2) * 12 + c * PR
            packed[at : at + PR, (s // 2) * 64 : (s // 2 + 1) * 64] = ring[rows]
    load_ref[...] = packed[...].astype(BF)


def relax_kernel(got_ref, own_ref, flow_out, mesh_out, raw, flow, coef, state, speed):
    gx, gy, sa = [lax.axis_index(a) for a in AXES]
    nx, ny, ns = [lax.axis_size(a) for a in AXES]
    shape = (24, 128)
    lane = lax.broadcasted_iota(jnp.int32, shape, 1)
    row = lax.broadcasted_iota(jnp.int32, shape, 0)
    low = lane < 64
    for c in range(3):
        for i in range(2):
            for k in range(ns):
                raw[c, i, k, 20:, :] = jnp.zeros((4, 128), F32)
    for g in range(5):
        chip = (gy + g) // 2 - gy // 2 - 1
        pair = (chip < 0) == (gy // 2 % 2 == 1)
        chip = jnp.where(chip == 0, 0, jnp.where(pair, 1, 2))
        core = g % 2
        for k in range(ns):
            hop = sa ^ k
            block = got_ref[hop ^ (hop // 2), chip, core].astype(F32)
            for i in range(2):
                for c in range(3):
                    raw[c, i, k, g * PR : (g + 1) * PR, :] = block[
                        i * 12 + c * PR : i * 12 + (c + 1) * PR
                    ]

    place = gy * PR - 2 * PR + row
    column = gx * 32 - 16 + lane % 64
    ok = (place >= 0) & (place < ny * PR) & (row < 5 * PR) & (column >= 0) & (column < nx * 32)
    inside = jnp.where(ok, 1.0, 0.0)
    edges = jnp.where(place == 0, 1.0, 0.0) + jnp.where(place == ny * PR - 1, 1.0, 0.0)
    edges += jnp.where(column == 0, 1.0, 0.0) + jnp.where(column == nx * 32 - 1, 1.0, 0.0)
    degree = 4.0 - edges
    zero = jnp.zeros(shape, F32)

    swapped = (row % PR >= 2) & low
    for c in range(2):
        carry = zero
        for k in range(ns):
            even = jnp.where(swapped, raw[c, 0, (k + ns - 1) % ns], raw[c, 0, k]) * inside
            odd = raw[c, 1, k] * inside
            flow[c, 0, k] = even
            flow[c, 1, k] = odd
            pair = even + odd
            turned = pltpu.roll(pair, 64, 1)
            even = even + jnp.where(low, 0.0, turned) + carry
            state[0, c, 0, k] = even
            state[0, c, 1, k] = even + odd
            carry = carry + pair + turned
            speed[c, 0, k] = zero
            speed[c, 1, k] = zero

    def below(get, i, k):
        if i == 1:
            return get(0, k)
        return pltpu.roll(jnp.where(low, get(1, k), get(1, k - 1) if k else 0.0), 64, 1)

    def above(get, i, k):
        if i == 0:
            return get(1, k)
        return pltpu.roll(jnp.where(low, get(0, k + 1) if k + 1 < ns else 0.0, get(0, k)), 64, 1)

    plane = inside * (step_size * spring_plane)
    stack = inside * (step_size * spring_stack)
    for i in range(2):
        for k in range(ns):
            w = raw[2, i, k] * stack
            w_next = above(lambda i, k: raw[2, i, k], i, k) * stack
            coef[0, i, k] = w
            coef[1, i, k] = w_next
            coef[2, i, k] = degree * plane + w + w_next
            for c in range(2):
                get = lambda i, k: flow[c, i, k]
                coef[3 + c, i, k] = w * get(i, k) - w_next * above(get, i, k)

    def advance(src, dst):
        for c in range(2):
            get = lambda i, k: state[src, c, i, k]
            for k in range(ns):
                for i in range(2):
                    m = get(i, k)
                    around = pltpu.roll(m, 1, 1) + pltpu.roll(m, 127, 1)
                    around += pltpu.roll(m, 1, 0) + pltpu.roll(m, 23, 0)
                    v = damping * speed[c, i, k] - coef[2, i, k] * m + plane * around
                    v += coef[0, i, k] * below(get, i, k) + coef[1, i, k] * above(get, i, k)
                    v += coef[3 + c, i, k]
                    speed[c, i, k] = v
                    state[dst, c, i, k] = m + v

    def two(step, unused):
        advance(0, 1)
        advance(1, 0)
        return unused

    lax.fori_loop(0, RELAX // 2, two, 0)
    mine = slice(2 * PR, 3 * PR)
    late = lax.broadcasted_iota(jnp.int32, (PR, 32), 0) >= 2
    for c in range(2):
        for s in range(4):
            lanes = slice((s // 2) * 64 + 16, (s // 2) * 64 + 48)
            mesh_out[s, c] = state[0, c, s % 2, sa][mine, lanes]
            f = own_ref[c * PR : (c + 1) * PR, s * 32 : (s + 1) * 32]
            if s == 0:
                f = jnp.where(late, flow[c, 0, sa][mine, lanes], f)
            flow_out[s, c] = f


PAIR = {0: 1, 1: 0, 2: 3, 3: 2}
CROSS = {1: 2, 2: 1}
RING = {1: 2, 2: 1, 0: 3, 3: 0}
SKIP = {0: 2, 2: 0, 1: 3, 3: 1}


def trade(array, axis, partner):
    sizes = [lax.axis_size(a) for a in AXES]
    route = []
    for x, y, k in np.ndindex(*sizes):
        place = {"gx": x, "chip": y // 2, "sa": k}
        target = (x, y ^ 1, k)
        if place[axis] in partner:
            place[axis] = partner[place[axis]]
            target = (place["gx"], place["chip"] * 2 + y % 2, place["sa"])
        route.append((
            int(np.ravel_multi_index((x, y, k), sizes)),
            int(np.ravel_multi_index(target, sizes)),
        ))
    return lax.ppermute(array, AXES, route)


def spread(load):
    near = trade(load, "gx", PAIR)
    far = trade(load, "gx", CROSS)
    odd = lax.axis_index("gx") % 2 == 1
    place = lax.broadcasted_iota(jnp.int32, load.shape, 1) % 64
    side = jnp.where((place < 16) == odd, near, far)
    load = jnp.where((place >= 16) & (place < 48), load, side)
    load = jnp.stack([load, trade(load, "gx", {})])
    near = trade(load, "chip", PAIR)
    far = trade(load, "chip", CROSS)
    load = jnp.stack([load, near, far])
    one = trade(load, "sa", PAIR)
    two = trade(load, "sa", RING)
    three = trade(load, "sa", SKIP)
    return jnp.stack([load, one, two, three])


def per_device(pixels, peak_offsets, validity):
    count, height, breadth = pixels.shape
    blocks = breadth // LANES
    size = lax.axis_size("sa")
    half = height // 2
    vmem = lambda: pl.BlockSpec(memory_space=pltpu.VMEM)
    held = pltpu.with_memory_space_constraint(pixels, pltpu.HBM)
    up, down, extra = pl.pallas_call(
        send_kernel,
        in_specs=[pl.BlockSpec(memory_space=pltpu.HBM)] * 2,
        out_specs=[vmem()] * 3,
        out_shape=[
            jax.ShapeDtypeStruct((half, breadth), BF),
            jax.ShapeDtypeStruct((half, breadth), BF),
            jax.ShapeDtypeStruct((8, 128), BF),
        ],
        scratch_shapes=[
            pltpu.VMEM((2, PR, 32), jnp.int32),
            pltpu.VMEM((8, 128), F32),
            pltpu.SemaphoreType.DMA((3,)),
        ],
        compiler_params=pltpu.CompilerParams(vmem_limit_bytes=GRANT),
        name="send",
    )(held, pltpu.with_memory_space_constraint(peak_offsets, pltpu.HBM))
    rise = [(i, (i + 1) % size) for i in range(size)]
    sink = [(i, (i - 1) % size) for i in range(size)]
    up = lax.ppermute(up, "sa", rise)
    down = lax.ppermute(down, "sa", sink)
    extra = lax.ppermute(extra, "sa", sink)

    rows = jnp.asarray(row_matrix())
    cols = jnp.asarray(col_matrix())
    second = jnp.asarray(second_matrix(blocks))
    whole = lambda shape: pl.BlockSpec(shape, lambda j: (0,) * len(shape))
    table_specs = [
        whole((2 * KROWS, PR * PATCH)),
        whole((256, 256)),
        whole((64, 2 * KROWS)),
        pl.BlockSpec((1, 2 * LANES, 8 * blocks * HELD), lambda j: (j, 0, 0)),
    ]
    inner, mix = pl.pallas_call(
        inner_kernel,
        grid=(blocks,),
        in_specs=[pl.BlockSpec((count, height, LANES), lambda j: (0, 0, j))] + table_specs,
        out_specs=[
            whole((96, 256)),
            pl.BlockSpec((2 * KROWS, LANES), lambda j: (0, j)),
        ],
        out_shape=[
            jax.ShapeDtypeStruct((96, 256), F32),
            jax.ShapeDtypeStruct((2 * KROWS, breadth), BF),
        ],
        compiler_params=pltpu.CompilerParams(dimension_semantics=("arbitrary",), vmem_limit_bytes=GRANT),
        cost_estimate=pl.CostEstimate(
            flops=8 * 10**9, bytes_accessed=8 * 2**20, transcendentals=10**6
        ),
        name="inner",
    )(
        held, rows, cols, jnp.asarray(first_matrix(False)), second,
    )

    own, load = pl.pallas_call(
        edge_kernel,
        in_specs=[vmem()] * 11,
        out_specs=[vmem(), vmem()],
        out_shape=[
            jax.ShapeDtypeStruct((8, 128), F32),
            jax.ShapeDtypeStruct((24, 128), BF),
        ],
        scratch_shapes=[
            pltpu.VMEM((SPAN, 16, 256), F32),
            pltpu.VMEM((2, 16, 32), jnp.int32),
            pltpu.VMEM((24, 128), F32),
        ],
        compiler_params=pltpu.CompilerParams(vmem_limit_bytes=GRANT),
        name="edge",
    )(
        up, down, extra, mix, rows, cols, jnp.asarray(first_matrix(True)), second,
        inner, peak_offsets, validity,
    )

    got = spread(load)

    field = (count, 2, PR, 32)
    stack = (2, size, 24, 128)
    return pl.pallas_call(
        relax_kernel,
        in_specs=[vmem(), vmem()],
        out_specs=[vmem(), vmem()],
        out_shape=[jax.ShapeDtypeStruct(field, F32)] * 2,
        scratch_shapes=[
            pltpu.VMEM((3,) + stack, F32),
            pltpu.VMEM((2,) + stack, F32),
            pltpu.VMEM((5,) + stack, F32),
            pltpu.VMEM((2, 2) + stack, F32),
            pltpu.VMEM((2,) + stack, F32),
        ],
        compiler_params=pltpu.CompilerParams(vmem_limit_bytes=GRANT),
        name="relax",
    )(got, own)


def solution(mesh):
    return jax.shard_map(
        per_device,
        mesh=mesh,
        in_specs=(P("sa", "gy", "gx"), P("sa", None, "gy", "gx"), P("sa", "gy", "gx")),
        out_specs=(P("sa", None, "gy", "gx"), P("sa", None, "gy", "gx")),
        check_vma=False,
    )
```

```python
import math

import jax
import jax.numpy as jnp
import numpy as np
from jax import lax
from jax.experimental import pallas as pl
from jax.experimental.pallas import tpu as pltpu
from jax.sharding import PartitionSpec as P


PATCH = 64
RELAX = 8
HALF = PATCH // 2 + 1
PR = 4
KROWS = 144
LANES = 512
SUB = LANES // 128
HELD = LANES // PATCH
REACH = 3
SPAN = 2 * REACH + 1
GRANT = 20 * 2**20
AXES = ("gx", "gy", "sa")

spring_plane = 0.5
spring_stack = 1.0
step_size = 0.2
damping = 0.6
whiten_floor = 1024.0

BF = jnp.bfloat16
F32 = jnp.float32


def wave_tables():
    angles = np.arange(PATCH, dtype=np.float32) * np.float32(2.0 * math.pi / PATCH)
    cosine = np.cos(angles).astype(BF).astype(np.float32)
    sine = np.sin(angles).astype(BF).astype(np.float32)
    return cosine, sine


def row_matrix():
    cosine, sine = wave_tables()
    out = np.zeros((2, KROWS, PR * PATCH), np.float32)
    phase = np.arange(HALF)[:, None] * np.arange(PATCH)[None, :] % PATCH
    for pr in range(PR):
        rows = slice(pr * HALF, (pr + 1) * HALF)
        cols = slice(pr * PATCH, (pr + 1) * PATCH)
        out[0, rows, cols] = cosine[phase]
        out[1, rows, cols] = -sine[phase]
    return out.reshape(2 * KROWS, PR * PATCH).astype(BF)


def col_matrix():
    cosine, sine = wave_tables()
    phase = np.arange(PATCH)[:, None] * np.arange(PATCH)[None, :] % PATCH
    out = np.zeros((2, 2, PATCH, 2, 2, PATCH), np.float32)
    for p in range(2):
        out[0, p, :, 0, p] = cosine[phase]
        out[1, p, :, 0, p] = sine[phase]
        out[0, p, :, 1, p] = -sine[phase]
        out[1, p, :, 1, p] = cosine[phase]
    return out.reshape(256, 256).astype(BF)


def first_matrix(flip):
    cosine, sine = wave_tables()
    out = np.zeros((2, 32, 2, KROWS), np.float32)
    k1 = np.arange(HALF)
    weight = np.where((k1 == 0) | (k1 == PATCH // 2), 1.0, 2.0)
    for p1 in range(SPAN):
        phase = k1 * (p1 - REACH) % PATCH
        for pr in range(PR):
            sign = -1.0 if flip and pr >= PR // 2 else 1.0
            row, cols = p1 * PR + pr, slice(pr * HALF, (pr + 1) * HALF)
            out[0, row, 0, cols] = weight * cosine[phase]
            out[0, row, 1, cols] = -sign * weight * sine[phase]
            out[1, row, 0, cols] = weight * sine[phase]
            out[1, row, 1, cols] = sign * weight * cosine[phase]
    return out.reshape(64, 2 * KROWS).astype(BF)


def second_matrix(blocks):
    cosine, sine = wave_tables()
    out = np.zeros((blocks, 2, HELD, PATCH, 8, blocks, HELD), np.float32)
    k2 = np.arange(PATCH)
    for p2 in range(SPAN):
        phase = k2 * (p2 - REACH) % PATCH
        for j in range(blocks):
            for p in range(HELD):
                out[j, 0, p, :, p2, j, p] = cosine[phase]
                out[j, 1, p, :, p2, j, p] = -sine[phase]
    return out.reshape(blocks, 2 * LANES, 8 * blocks * HELD).astype(BF)


def whiten(now, old):
    real, imag = [], []
    for (now_real, now_imag), (old_real, old_imag) in zip(now, old):
        cross_real = now_real * old_real + now_imag * old_imag
        cross_imag = now_imag * old_real - now_real * old_imag
        power = cross_real * cross_real + cross_imag * cross_imag
        inverse = lax.rsqrt(power + whiten_floor * whiten_floor)
        real.append((cross_real * inverse).astype(BF))
        imag.append((cross_imag * inverse).astype(BF))
    return jnp.concatenate(
        [jnp.concatenate(real, axis=1), jnp.concatenate(imag, axis=1)], axis=0
    )


def first_sum(table_ref, prod):
    both = jnp.dot(table_ref[...], prod, preferred_element_type=F32)
    return jnp.concatenate([both[:32], both[32:]], axis=1)


def send_kernel(px_ref, offs_ref, up_ref, down_ref, extra_ref, offs, low, sems):
    half = up_ref.shape[0]
    last = px_ref.shape[0] - 1
    copies = [
        pltpu.make_async_copy(offs_ref.at[0], offs, sems.at[0]),
        pltpu.make_async_copy(px_ref.at[last, pl.ds(0, half)], up_ref, sems.at[1]),
        pltpu.make_async_copy(px_ref.at[0, pl.ds(half, half)], down_ref, sems.at[2]),
    ]
    for copy in copies:
        copy.start()
    low[...] = jnp.zeros_like(low)
    copies[0].wait()
    for c in range(2):
        low[c * 2 : c * 2 + 2, :32] = offs[c, 2:4].astype(F32)
    extra_ref[...] = low[...].astype(BF)
    for copy in copies[1:]:
        copy.wait()


def row_sum(strips, rows_ref):
    return jnp.dot(rows_ref[...], strips, preferred_element_type=F32).astype(BF)


def col_sum(half, cols_ref):
    both = []
    for b in range(SUB):
        lanes = slice(b * 128, (b + 1) * 128)
        both.append(jnp.concatenate([half[:KROWS, lanes], half[KROWS:, lanes]], axis=1))
    spec = jnp.dot(jnp.concatenate(both, axis=0), cols_ref[...], preferred_element_type=F32)
    out = []
    for b in range(SUB):
        rows = slice(b * KROWS, (b + 1) * KROWS)
        out.append((spec[rows, :128], spec[rows, 128:]))
    return out


def inner_kernel(px_ref, rows_ref, cols_ref, first_ref, second_ref, corr_ref, mix_ref):
    count = px_ref.shape[0]
    sums, specs = [], []
    half = row_sum(px_ref[0], rows_ref)
    prod = None
    for s in range(count):
        specs.append(col_sum(half, cols_ref))
        if s + 1 < count:
            half = row_sum(px_ref[s + 1], rows_ref)
        if prod is not None:
            sums.append(first_sum(first_ref, prod).astype(BF))
        prod = whiten(specs[s], specs[s - 1]) if s else None
    sums.append(first_sum(first_ref, prod).astype(BF))
    edge, old = specs[0], specs[-1]
    low = lax.broadcasted_iota(jnp.int32, (KROWS, 128), 0) < 2 * HALF
    for b in range(SUB):
        for part in range(2):
            mix_ref[part * KROWS : (part + 1) * KROWS, b * 128 : (b + 1) * 128] = jnp.where(
                low, edge[b][part], old[b][part]
            ).astype(BF)
    term = jnp.dot(jnp.concatenate(sums, axis=0), second_ref[0], preferred_element_type=F32)

    @pl.when(pl.program_id(0) == 0)
    def _():
        corr_ref[...] = term

    @pl.when(pl.program_id(0) > 0)
    def _():
        corr_ref[...] += term


def pick(pieces, offset):
    value = pieces[0]
    for i in range(1, 5):
        value = jnp.where(offset == i - 2, pieces[i], value)
    return value


def peak_step(low, center, high):
    bend = jnp.maximum(jnp.abs(low - 2.0 * center + high), 1.0)
    return (low - high) / (2.0 * bend)


def edge_kernel(
    up_ref, down_ref, extra_ref, mix_ref, rows_ref, cols_ref, first_ref, second_ref,
    inner_ref, offs_ref, valid_ref, flow_ref, load_ref, picked, offs, packed,
):
    sa = lax.axis_index("sa")
    breadth = mix_ref.shape[1]
    pr = lax.broadcasted_iota(jnp.int32, (32, 2 * LANES), 0) % PR
    dropped = ((sa == 0) & (pr < 2)) | ((sa == lax.axis_size("sa") - 1) & (pr >= 2))

    def strips(j):
        lanes = slice(j * LANES, (j + 1) * LANES)
        return jnp.concatenate([up_ref[:, lanes], down_ref[:, lanes]], axis=0)

    blocks = breadth // LANES
    corr = jnp.zeros((32, 256), F32)
    row = row_sum(strips(0), rows_ref)
    prod = None
    for j in range(blocks + 1):
        if j < blocks:
            there = col_sum(row, cols_ref)
            if j + 1 < blocks:
                row = row_sum(strips(j + 1), rows_ref)
        if j:
            sums = first_sum(first_ref, prod)
            sums = jnp.where(dropped, 0.0, sums).astype(BF)
            corr += jnp.dot(sums, second_ref[j - 1], preferred_element_type=F32)
        if j < blocks:
            here = []
            for b in range(SUB * j, SUB * (j + 1)):
                part = slice(b * 128, (b + 1) * 128)
                here.append((mix_ref[:KROWS, part].astype(F32), mix_ref[KROWS:, part].astype(F32)))
            prod = whiten(here, there)

    for p1 in range(SPAN):
        picked[p1, 0:PR] = corr[p1 * PR : (p1 + 1) * PR]
        for s in range(3):
            picked[p1, (s + 1) * PR : (s + 2) * PR] = inner_ref[
                s * 32 + p1 * PR : s * 32 + (p1 + 1) * PR
            ]
    extra = extra_ref[...].astype(F32).astype(jnp.int32)
    for c in range(2):
        for s in range(4):
            offs[c, s * PR : (s + 1) * PR, :] = offs_ref[s, c]
        offs[c, 2:4, :] = extra[c * 2 : c * 2 + 2, :32]
    row_off, col_off = offs[0], offs[1]
    wide = jnp.concatenate([row_off] * 8, axis=1)
    layers = [picked[p1] * (1.0 / PATCH) for p1 in range(SPAN)]
    low, mid, high = [pick(layers[d : d + 5], wide) for d in range(3)]

    def cut(layer, d):
        return pick([layer[:, (d + i) * 32 : (d + i + 1) * 32] for i in range(5)], col_off)

    center = cut(mid, 1)
    flows = (
        row_off.astype(F32) + peak_step(cut(low, 1), center, cut(high, 1)),
        col_off.astype(F32) + peak_step(cut(mid, 0), center, cut(mid, 2)),
    )
    weights = jnp.concatenate([valid_ref[s].astype(F32) for s in range(4)], axis=0)
    for c, field in enumerate(flows + (weights,)):
        ring = jnp.concatenate([field[:, 16:], field, field[:, :16]], axis=1)
        for s in range(4):
            rows = slice(s * PR, (s + 1) * PR)
            if c < 2:
                flow_ref[c * PR : (c + 1) * PR, s * 32 : (s + 1) * 32] = field[rows]
            at = (s % 2) * 12 + c * PR
            packed[at : at + PR, (s // 2) * 64 : (s // 2 + 1) * 64] = ring[rows]
    load_ref[...] = packed[...].astype(BF)


def relax_kernel(got_ref, own_ref, flow_out, mesh_out, raw, flow, coef, state):
    gx, gy, sa = [lax.axis_index(a) for a in AXES]
    nx, ny, ns = [lax.axis_size(a) for a in AXES]
    shape = (24, 128)
    lane = lax.broadcasted_iota(jnp.int32, shape, 1)
    row = lax.broadcasted_iota(jnp.int32, shape, 0)
    low = lane < 64
    for c in range(3):
        for i in range(2):
            for k in range(ns):
                raw[c, i, k, 20:, :] = jnp.zeros((4, 128), F32)
    for g in range(5):
        chip = (gy + g) // 2 - gy // 2 - 1
        pair = (chip < 0) == (gy // 2 % 2 == 1)
        chip = jnp.where(chip == 0, 0, jnp.where(pair, 1, 2))
        core = g % 2
        for k in range(ns):
            hop = sa ^ k
            block = got_ref[hop ^ (hop // 2), chip, core].astype(F32)
            for i in range(2):
                for c in range(3):
                    raw[c, i, k, g * PR : (g + 1) * PR, :] = block[
                        i * 12 + c * PR : i * 12 + (c + 1) * PR
                    ]

    place = gy * PR - 2 * PR + row
    column = gx * 32 - 16 + lane % 64
    ok = (place >= 0) & (place < ny * PR) & (row < 5 * PR) & (column >= 0) & (column < nx * 32)
    inside = jnp.where(ok, 1.0, 0.0)
    edges = jnp.where(place == 0, 1.0, 0.0) + jnp.where(place == ny * PR - 1, 1.0, 0.0)
    edges += jnp.where(column == 0, 1.0, 0.0) + jnp.where(column == nx * 32 - 1, 1.0, 0.0)
    degree = 4.0 - edges
    zero = jnp.zeros(shape, F32)

    blank = (0, 1, ns + 2, ns + 3)
    for k in blank:
        for i in range(2):
            for c in range(2):
                state[0, c, i, k] = zero
                state[1, c, i, k] = zero
            if k in (1, ns + 2):
                for c in range(5):
                    coef[c, i, k] = zero

    swapped = (row % PR >= 2) & low
    for c in range(2):
        carry = zero
        for k in range(ns):
            even = jnp.where(swapped, raw[c, 0, (k + ns - 1) % ns], raw[c, 0, k]) * inside
            odd = raw[c, 1, k] * inside
            flow[c, 0, k] = even
            flow[c, 1, k] = odd
            pair = even + odd
            turned = pltpu.roll(pair, 64, 1)
            even = even + jnp.where(low, 0.0, turned) + carry
            odd = even + odd
            for old in range(2):
                state[old, c, 0, k + 2] = even
                state[old, c, 1, k + 2] = odd
            carry = carry + pair + turned

    def turn(array):
        return pltpu.roll(array, 64, 1)

    plane = inside * (step_size * spring_plane)
    stack = inside * (step_size * spring_stack)
    for k in range(ns):
        weights = [raw[2, i, k] * stack for i in range(2)]
        later = raw[2, 0, k + 1] * stack if k + 1 < ns else 0.0
        nexts = [weights[1], turn(jnp.where(low, later, weights[0]))]
        for i in range(2):
            coef[0, i, k + 2] = weights[i]
            coef[1, i, k + 2] = nexts[i]
            coef[2, i, k + 2] = 1.0 + damping - degree * plane - weights[i] - nexts[i]
        for c in range(2):
            later = flow[c, 0, k + 1] if k + 1 < ns else 0.0
            ahead = [flow[c, 1, k], turn(jnp.where(low, later, flow[c, 0, k]))]
            for i in range(2):
                coef[3 + c, i, k + 2] = weights[i] * flow[c, i, k] - nexts[i] * ahead[i]

    def advance(step, c, k):
        src, dst = (step + 1) % 2, step % 2
        top = 8 if step == RELAX else 0
        end = 24 if step < 4 else 16
        rows, read = slice(top, end), slice(0, end)
        now = [state[src, c, i, k, read] for i in range(2)]
        here = [m[rows] for m in now]
        edge = low[rows]
        behind = [
            turn(jnp.where(edge, here[1], state[src, c, 1, k - 1, rows])),
            here[0],
        ]
        ahead = [
            here[1],
            turn(jnp.where(edge, state[src, c, 0, k + 1, rows], here[0])),
        ]
        done = []
        for i in range(2):
            around = pltpu.roll(here[i], 1, 1) + pltpu.roll(here[i], 127, 1)
            around += pltpu.roll(now[i], 1, 0)[rows]
            if step == 4:
                around += pltpu.roll(state[src, c, i, k], 23, 0)[rows]
            else:
                around += pltpu.roll(now[i], end - 1, 0)[rows]
            m = coef[2, i, k, rows] * here[i] - damping * state[dst, c, i, k, rows]
            m += plane[rows] * around + coef[3 + c, i, k, rows]
            m += coef[0, i, k, rows] * behind[i] + coef[1, i, k, rows] * ahead[i]
            if step < RELAX:
                state[dst, c, i, k, rows] = m
            done.append(m)
        return done

    for step in range(1, 4):
        for c in range(2):
            for k in range(ns):
                advance(step, c, k + 2)
    for step in range(4, RELAX):
        for c in range(2):
            for d in range(3):
                advance(step, c, sa + d + 1)
    mine = slice(2 * PR, 3 * PR)
    late = lax.broadcasted_iota(jnp.int32, (PR, 32), 0) >= 2
    for c in range(2):
        final = advance(RELAX, c, sa + 2)
        for s in range(4):
            lanes = slice((s // 2) * 64 + 16, (s // 2) * 64 + 48)
            mesh_out[s, c] = final[s % 2][:PR, lanes]
            f = own_ref[c * PR : (c + 1) * PR, s * 32 : (s + 1) * 32]
            if s == 0:
                f = jnp.where(late, flow[c, 0, sa][mine, lanes], f)
            flow_out[s, c] = f


PAIR = {0: 1, 1: 0, 2: 3, 3: 2}
CROSS = {1: 2, 2: 1}
RING = {1: 2, 2: 1, 0: 3, 3: 0}
SKIP = {0: 2, 2: 0, 1: 3, 3: 1}


def trade(array, axis, partner):
    sizes = [lax.axis_size(a) for a in AXES]
    route = []
    for x, y, k in np.ndindex(*sizes):
        place = {"gx": x, "chip": y // 2, "sa": k}
        target = (x, y ^ 1, k)
        if place[axis] in partner:
            place[axis] = partner[place[axis]]
            target = (place["gx"], place["chip"] * 2 + y % 2, place["sa"])
        route.append((
            int(np.ravel_multi_index((x, y, k), sizes)),
            int(np.ravel_multi_index(target, sizes)),
        ))
    return lax.ppermute(array, AXES, route)


def spread(load):
    near = trade(load, "gx", PAIR)
    far = trade(load, "gx", CROSS)
    odd = lax.axis_index("gx") % 2 == 1
    place = lax.broadcasted_iota(jnp.int32, load.shape, 1) % 64
    side = jnp.where((place < 16) == odd, near, far)
    load = jnp.where((place >= 16) & (place < 48), load, side)
    load = jnp.stack([load, trade(load, "gx", {})])
    near = trade(load, "chip", PAIR)
    far = trade(load, "chip", CROSS)
    load = jnp.stack([load, near, far])
    one = trade(load, "sa", PAIR)
    two = trade(load, "sa", RING)
    three = trade(load, "sa", SKIP)
    return jnp.stack([load, one, two, three])


def per_device(pixels, peak_offsets, validity):
    count, height, breadth = pixels.shape
    blocks = breadth // LANES
    size = lax.axis_size("sa")
    half = height // 2
    vmem = lambda: pl.BlockSpec(memory_space=pltpu.VMEM)
    held = pltpu.with_memory_space_constraint(pixels, pltpu.HBM)
    up, down, extra = pl.pallas_call(
        send_kernel,
        in_specs=[pl.BlockSpec(memory_space=pltpu.HBM)] * 2,
        out_specs=[vmem()] * 3,
        out_shape=[
            jax.ShapeDtypeStruct((half, breadth), BF),
            jax.ShapeDtypeStruct((half, breadth), BF),
            jax.ShapeDtypeStruct((8, 128), BF),
        ],
        scratch_shapes=[
            pltpu.VMEM((2, PR, 32), jnp.int32),
            pltpu.VMEM((8, 128), F32),
            pltpu.SemaphoreType.DMA((3,)),
        ],
        compiler_params=pltpu.CompilerParams(vmem_limit_bytes=GRANT),
        name="send",
    )(held, pltpu.with_memory_space_constraint(peak_offsets, pltpu.HBM))
    rise = [(i, (i + 1) % size) for i in range(size)]
    sink = [(i, (i - 1) % size) for i in range(size)]
    up = lax.ppermute(up, "sa", rise)
    down = lax.ppermute(down, "sa", sink)
    extra = lax.ppermute(extra, "sa", sink)

    rows = jnp.asarray(row_matrix())
    cols = jnp.asarray(col_matrix())
    second = jnp.asarray(second_matrix(blocks))
    whole = lambda shape: pl.BlockSpec(shape, lambda j: (0,) * len(shape))
    table_specs = [
        whole((2 * KROWS, PR * PATCH)),
        whole((256, 256)),
        whole((64, 2 * KROWS)),
        pl.BlockSpec((1, 2 * LANES, 8 * blocks * HELD), lambda j: (j, 0, 0)),
    ]
    inner, mix = pl.pallas_call(
        inner_kernel,
        grid=(blocks,),
        in_specs=[pl.BlockSpec((count, height, LANES), lambda j: (0, 0, j))] + table_specs,
        out_specs=[
            whole((96, 256)),
            pl.BlockSpec((2 * KROWS, LANES), lambda j: (0, j)),
        ],
        out_shape=[
            jax.ShapeDtypeStruct((96, 256), F32),
            jax.ShapeDtypeStruct((2 * KROWS, breadth), BF),
        ],
        compiler_params=pltpu.CompilerParams(dimension_semantics=("arbitrary",), vmem_limit_bytes=GRANT),
        cost_estimate=pl.CostEstimate(
            flops=8 * 10**9, bytes_accessed=8 * 2**20, transcendentals=10**6
        ),
        name="inner",
    )(
        held, rows, cols, jnp.asarray(first_matrix(False)), second,
    )

    own, load = pl.pallas_call(
        edge_kernel,
        in_specs=[vmem()] * 11,
        out_specs=[vmem(), vmem()],
        out_shape=[
            jax.ShapeDtypeStruct((8, 128), F32),
            jax.ShapeDtypeStruct((24, 128), BF),
        ],
        scratch_shapes=[
            pltpu.VMEM((SPAN, 16, 256), F32),
            pltpu.VMEM((2, 16, 32), jnp.int32),
            pltpu.VMEM((24, 128), F32),
        ],
        compiler_params=pltpu.CompilerParams(vmem_limit_bytes=GRANT),
        name="edge",
    )(
        up, down, extra, mix, rows, cols, jnp.asarray(first_matrix(True)), second,
        inner, peak_offsets, validity,
    )

    got = spread(load)

    field = (count, 2, PR, 32)
    stack = (2, size, 24, 128)
    return pl.pallas_call(
        relax_kernel,
        in_specs=[vmem(), vmem()],
        out_specs=[vmem(), vmem()],
        out_shape=[jax.ShapeDtypeStruct(field, F32)] * 2,
        scratch_shapes=[
            pltpu.VMEM((3,) + stack, F32),
            pltpu.VMEM((2,) + stack, F32),
            pltpu.VMEM((5, 2, size + 4, 24, 128), F32),
            pltpu.VMEM((2, 2, 2, size + 4, 24, 128), F32),
        ],
        compiler_params=pltpu.CompilerParams(vmem_limit_bytes=GRANT),
        name="relax",
    )(got, own)


def solution(mesh):
    return jax.shard_map(
        per_device,
        mesh=mesh,
        in_specs=(P("sa", "gy", "gx"), P("sa", None, "gy", "gx"), P("sa", "gy", "gx")),
        out_specs=(P("sa", None, "gy", "gx"), P("sa", None, "gy", "gx")),
        check_vma=False,
    )
```

```python
import math

import jax
import jax.numpy as jnp
import numpy as np
from jax import lax
from jax.experimental import pallas as pl
from jax.experimental.pallas import tpu as pltpu
from jax.sharding import PartitionSpec as P


PATCH = 64
RELAX = 8
HALF = PATCH // 2 + 1
PR = 4
KROWS = 144
LANES = 512
SUB = LANES // 128
HELD = LANES // PATCH
REACH = 3
SPAN = 2 * REACH + 1
GRANT = 20 * 2**20
AXES = ("gx", "gy", "sa")

spring_plane = 0.5
spring_stack = 1.0
step_size = 0.2
damping = 0.6
whiten_floor = 1024.0

BF = jnp.bfloat16
F32 = jnp.float32


def wave_tables():
    angles = np.arange(PATCH, dtype=np.float32) * np.float32(2.0 * math.pi / PATCH)
    cosine = np.cos(angles).astype(BF).astype(np.float32)
    sine = np.sin(angles).astype(BF).astype(np.float32)
    return cosine, sine


def row_matrix():
    cosine, sine = wave_tables()
    out = np.zeros((2, KROWS, PR * PATCH), np.float32)
    phase = np.arange(HALF)[:, None] * np.arange(PATCH)[None, :] % PATCH
    for pr in range(PR):
        rows = slice(pr * HALF, (pr + 1) * HALF)
        cols = slice(pr * PATCH, (pr + 1) * PATCH)
        out[0, rows, cols] = cosine[phase]
        out[1, rows, cols] = -sine[phase]
    return out.reshape(2 * KROWS, PR * PATCH).astype(BF)


def col_matrix():
    cosine, sine = wave_tables()
    phase = np.arange(PATCH)[:, None] * np.arange(PATCH)[None, :] % PATCH
    out = np.zeros((2, 2, PATCH, 2, 2, PATCH), np.float32)
    for p in range(2):
        out[0, p, :, 0, p] = cosine[phase]
        out[1, p, :, 0, p] = sine[phase]
        out[0, p, :, 1, p] = -sine[phase]
        out[1, p, :, 1, p] = cosine[phase]
    return out.reshape(256, 256).astype(BF)


def first_matrix(flip):
    cosine, sine = wave_tables()
    out = np.zeros((2, 32, 2, KROWS), np.float32)
    k1 = np.arange(HALF)
    weight = np.where((k1 == 0) | (k1 == PATCH // 2), 1.0, 2.0)
    for p1 in range(SPAN):
        phase = k1 * (p1 - REACH) % PATCH
        for pr in range(PR):
            sign = -1.0 if flip and pr >= PR // 2 else 1.0
            row, cols = p1 * PR + pr, slice(pr * HALF, (pr + 1) * HALF)
            out[0, row, 0, cols] = weight * cosine[phase]
            out[0, row, 1, cols] = -sign * weight * sine[phase]
            out[1, row, 0, cols] = weight * sine[phase]
            out[1, row, 1, cols] = sign * weight * cosine[phase]
    return out.reshape(64, 2 * KROWS).astype(BF)


def second_matrix(blocks):
    cosine, sine = wave_tables()
    out = np.zeros((blocks, 2, HELD, PATCH, 8, blocks, HELD), np.float32)
    k2 = np.arange(PATCH)
    for p2 in range(SPAN):
        phase = k2 * (p2 - REACH) % PATCH
        for j in range(blocks):
            for p in range(HELD):
                out[j, 0, p, :, p2, j, p] = cosine[phase]
                out[j, 1, p, :, p2, j, p] = -sine[phase]
    return out.reshape(blocks, 2 * LANES, 8 * blocks * HELD).astype(BF)


def whiten(now, old):
    real, imag = [], []
    for (now_real, now_imag), (old_real, old_imag) in zip(now, old):
        cross_real = now_real * old_real + now_imag * old_imag
        cross_imag = now_imag * old_real - now_real * old_imag
        power = cross_real * cross_real + cross_imag * cross_imag
        inverse = lax.rsqrt(power + whiten_floor * whiten_floor)
        real.append((cross_real * inverse).astype(BF))
        imag.append((cross_imag * inverse).astype(BF))
    return jnp.concatenate(
        [jnp.concatenate(real, axis=1), jnp.concatenate(imag, axis=1)], axis=0
    )


def first_sum(table_ref, prod):
    both = jnp.dot(table_ref[...], prod, preferred_element_type=F32)
    return jnp.concatenate([both[:32], both[32:]], axis=1)


def send_kernel(px_ref, offs_ref, up_ref, down_ref, extra_ref, offs, low, sems):
    half = up_ref.shape[0]
    last = px_ref.shape[0] - 1
    copies = [
        pltpu.make_async_copy(offs_ref.at[0], offs, sems.at[0]),
        pltpu.make_async_copy(px_ref.at[last, pl.ds(0, half)], up_ref, sems.at[1]),
        pltpu.make_async_copy(px_ref.at[0, pl.ds(half, half)], down_ref, sems.at[2]),
    ]
    for copy in copies:
        copy.start()
    low[...] = jnp.zeros_like(low)
    copies[0].wait()
    for c in range(2):
        low[c * 2 : c * 2 + 2, :32] = offs[c, 2:4].astype(F32)
    extra_ref[...] = low[...].astype(BF)
    for copy in copies[1:]:
        copy.wait()


def row_sum(strips, rows_ref):
    return jnp.dot(rows_ref[...], strips, preferred_element_type=F32).astype(BF)


def col_sum(half, cols_ref):
    both = []
    for b in range(SUB):
        lanes = slice(b * 128, (b + 1) * 128)
        both.append(jnp.concatenate([half[:KROWS, lanes], half[KROWS:, lanes]], axis=1))
    spec = jnp.dot(jnp.concatenate(both, axis=0), cols_ref[...], preferred_element_type=F32)
    out = []
    for b in range(SUB):
        rows = slice(b * KROWS, (b + 1) * KROWS)
        out.append((spec[rows, :128], spec[rows, 128:]))
    return out


def pick(pieces, offset):
    value = pieces[0]
    for i in range(1, 5):
        value = jnp.where(offset == i - 2, pieces[i], value)
    return value


def peak_step(low, center, high):
    bend = jnp.maximum(jnp.abs(low - 2.0 * center + high), 1.0)
    return (low - high) / (2.0 * bend)


def refine(layers, row_off, col_off):
    wide = jnp.concatenate([row_off] * 8, axis=1)
    low, mid, high = [pick(layers[d : d + 5], wide) for d in range(3)]

    def cut(layer, d):
        return pick([layer[:, (d + i) * 32 : (d + i + 1) * 32] for i in range(5)], col_off)

    center = cut(mid, 1)
    return (
        row_off.astype(F32) + peak_step(cut(low, 1), center, cut(high, 1)),
        col_off.astype(F32) + peak_step(cut(mid, 0), center, cut(mid, 2)),
    )


def lay(ref, c, s, field):
    ring = jnp.concatenate([field[:, 16:], field, field[:, :16]], axis=1)
    at = (s % 2) * 12 + c * PR
    ref[at : at + PR, (s // 2) * 64 : (s // 2 + 1) * 64] = ring


def inner_kernel(
    px_ref, rows_ref, cols_ref, first_ref, second_ref, offs_ref, valid_ref,
    flow_ref, load_ref, mix_ref, corr_ref, picked, offs,
):
    count = px_ref.shape[0]
    sums, specs = [], []
    half = row_sum(px_ref[0], rows_ref)
    prod = None
    for s in range(count):
        specs.append(col_sum(half, cols_ref))
        if s + 1 < count:
            half = row_sum(px_ref[s + 1], rows_ref)
        if prod is not None:
            sums.append(first_sum(first_ref, prod).astype(BF))
        prod = whiten(specs[s], specs[s - 1]) if s else None
    sums.append(first_sum(first_ref, prod).astype(BF))
    edge, old = specs[0], specs[-1]
    low = lax.broadcasted_iota(jnp.int32, (KROWS, 128), 0) < 2 * HALF
    for b in range(SUB):
        for part in range(2):
            mix_ref[part * KROWS : (part + 1) * KROWS, b * 128 : (b + 1) * 128] = jnp.where(
                low, edge[b][part], old[b][part]
            ).astype(BF)
    term = jnp.dot(jnp.concatenate(sums, axis=0), second_ref[0], preferred_element_type=F32)

    @pl.when(pl.program_id(0) == 0)
    def _():
        corr_ref[...] = term

    @pl.when(pl.program_id(0) > 0)
    def _():
        corr_ref[...] += term

    @pl.when(pl.program_id(0) == pl.num_programs(0) - 1)
    def _():
        flow_ref[...] = jnp.zeros_like(flow_ref)
        load_ref[...] = jnp.zeros_like(load_ref)
        for s in range(1, count):
            rows = slice((s - 1) * PR, s * PR)
            for p1 in range(SPAN):
                at = (s - 1) * 32 + p1 * PR
                picked[p1, rows] = corr_ref[at : at + PR] * (1.0 / PATCH)
            for c in range(2):
                offs[c, rows] = offs_ref[s, c]
        flows = refine([picked[p1] for p1 in range(SPAN)], offs[0], offs[1])
        for s in range(count):
            lay(load_ref, 2, s, valid_ref[s].astype(F32))
            for c in range(2 if s else 0):
                piece = flows[c][(s - 1) * PR : s * PR]
                lay(load_ref, c, s, piece)
                flow_ref[c * PR : (c + 1) * PR, s * 32 : (s + 1) * 32] = piece


def edge_kernel(
    up_ref, down_ref, extra_ref, mix_ref, rows_ref, cols_ref, first_ref, second_ref,
    inner_ref, ready_ref, offs_ref, flow_ref, load_ref, offs, packed,
):
    sa = lax.axis_index("sa")
    breadth = mix_ref.shape[1]
    pr = lax.broadcasted_iota(jnp.int32, (32, 2 * LANES), 0) % PR
    dropped = ((sa == 0) & (pr < 2)) | ((sa == lax.axis_size("sa") - 1) & (pr >= 2))

    def strips(j):
        lanes = slice(j * LANES, (j + 1) * LANES)
        return jnp.concatenate([up_ref[:, lanes], down_ref[:, lanes]], axis=0)

    blocks = breadth // LANES
    corr = jnp.zeros((32, 256), F32)
    row = row_sum(strips(0), rows_ref)
    prod = None
    for j in range(blocks + 1):
        if j < blocks:
            there = col_sum(row, cols_ref)
            if j + 1 < blocks:
                row = row_sum(strips(j + 1), rows_ref)
        if j:
            sums = first_sum(first_ref, prod)
            sums = jnp.where(dropped, 0.0, sums).astype(BF)
            corr += jnp.dot(sums, second_ref[j - 1], preferred_element_type=F32)
        if j < blocks:
            here = []
            for b in range(SUB * j, SUB * (j + 1)):
                part = slice(b * 128, (b + 1) * 128)
                here.append((mix_ref[:KROWS, part].astype(F32), mix_ref[KROWS:, part].astype(F32)))
            prod = whiten(here, there)

    extra = extra_ref[...].astype(F32).astype(jnp.int32)
    for c in range(2):
        offs[c] = offs_ref[0, c]
        offs[c, 2:4, :] = extra[c * 2 : c * 2 + 2, :32]
    layers = [corr[p1 * PR : (p1 + 1) * PR] * (1.0 / PATCH) for p1 in range(SPAN)]
    flows = refine(layers, offs[0], offs[1])
    flow_ref[...] = inner_ref[...]
    packed[...] = ready_ref[...]
    for c in range(2):
        flow_ref[c * PR : (c + 1) * PR, :32] = flows[c]
        lay(packed, c, 0, flows[c])
    load_ref[...] = packed[...].astype(BF)


def relax_kernel(got_ref, own_ref, flow_out, mesh_out, raw, flow, coef, state):
    gx, gy, sa = [lax.axis_index(a) for a in AXES]
    nx, ny, ns = [lax.axis_size(a) for a in AXES]
    shape = (24, 128)
    lane = lax.broadcasted_iota(jnp.int32, shape, 1)
    row = lax.broadcasted_iota(jnp.int32, shape, 0)
    low = lane < 64
    for c in range(3):
        for i in range(2):
            for k in range(ns):
                raw[c, i, k, 20:, :] = jnp.zeros((4, 128), F32)
    for g in range(5):
        chip = (gy + g) // 2 - gy // 2 - 1
        pair = (chip < 0) == (gy // 2 % 2 == 1)
        chip = jnp.where(chip == 0, 0, jnp.where(pair, 1, 2))
        core = g % 2
        for k in range(ns):
            hop = sa ^ k
            block = got_ref[hop ^ (hop // 2), chip, core].astype(F32)
            for i in range(2):
                for c in range(3):
                    raw[c, i, k, g * PR : (g + 1) * PR, :] = block[
                        i * 12 + c * PR : i * 12 + (c + 1) * PR
                    ]

    place = gy * PR - 2 * PR + row
    column = gx * 32 - 16 + lane % 64
    ok = (place >= 0) & (place < ny * PR) & (row < 5 * PR) & (column >= 0) & (column < nx * 32)
    inside = jnp.where(ok, 1.0, 0.0)
    edges = jnp.where(place == 0, 1.0, 0.0) + jnp.where(place == ny * PR - 1, 1.0, 0.0)
    edges += jnp.where(column == 0, 1.0, 0.0) + jnp.where(column == nx * 32 - 1, 1.0, 0.0)
    degree = 4.0 - edges
    zero = jnp.zeros(shape, F32)

    blank = (0, 1, ns + 2, ns + 3)
    for k in blank:
        for i in range(2):
            for c in range(2):
                state[0, c, i, k] = zero
                state[1, c, i, k] = zero
            if k in (1, ns + 2):
                for c in range(5):
                    coef[c, i, k] = zero

    swapped = (row % PR >= 2) & low
    for c in range(2):
        carry = zero
        for k in range(ns):
            even = jnp.where(swapped, raw[c, 0, (k + ns - 1) % ns], raw[c, 0, k]) * inside
            odd = raw[c, 1, k] * inside
            flow[c, 0, k] = even
            flow[c, 1, k] = odd
            pair = even + odd
            turned = pltpu.roll(pair, 64, 1)
            even = even + jnp.where(low, 0.0, turned) + carry
            odd = even + odd
            for old in range(2):
                state[old, c, 0, k + 2] = even
                state[old, c, 1, k + 2] = odd
            carry = carry + pair + turned

    def turn(array):
        return pltpu.roll(array, 64, 1)

    plane = inside * (step_size * spring_plane)
    stack = inside * (step_size * spring_stack)
    for k in range(ns):
        weights = [raw[2, i, k] * stack for i in range(2)]
        later = raw[2, 0, k + 1] * stack if k + 1 < ns else 0.0
        nexts = [weights[1], turn(jnp.where(low, later, weights[0]))]
        for i in range(2):
            coef[0, i, k + 2] = weights[i]
            coef[1, i, k + 2] = nexts[i]
            coef[2, i, k + 2] = 1.0 + damping - degree * plane - weights[i] - nexts[i]
        for c in range(2):
            later = flow[c, 0, k + 1] if k + 1 < ns else 0.0
            ahead = [flow[c, 1, k], turn(jnp.where(low, later, flow[c, 0, k]))]
            for i in range(2):
                coef[3 + c, i, k + 2] = weights[i] * flow[c, i, k] - nexts[i] * ahead[i]

    def advance(step, c, k):
        src, dst = (step + 1) % 2, step % 2
        top = 8 if step == RELAX else 0
        end = 24 if step < 4 else 16
        rows, read = slice(top, end), slice(0, end)
        now = [state[src, c, i, k, read] for i in range(2)]
        here = [m[rows] for m in now]
        edge = low[rows]
        behind = [
            turn(jnp.where(edge, here[1], state[src, c, 1, k - 1, rows])),
            here[0],
        ]
        ahead = [
            here[1],
            turn(jnp.where(edge, state[src, c, 0, k + 1, rows], here[0])),
        ]
        done = []
        for i in range(2):
            around = pltpu.roll(here[i], 1, 1) + pltpu.roll(here[i], 127, 1)
            around += pltpu.roll(now[i], 1, 0)[rows]
            if step == 4:
                around += pltpu.roll(state[src, c, i, k], 23, 0)[rows]
            else:
                around += pltpu.roll(now[i], end - 1, 0)[rows]
            m = coef[2, i, k, rows] * here[i] - damping * state[dst, c, i, k, rows]
            m += plane[rows] * around + coef[3 + c, i, k, rows]
            m += coef[0, i, k, rows] * behind[i] + coef[1, i, k, rows] * ahead[i]
            if step < RELAX:
                state[dst, c, i, k, rows] = m
            done.append(m)
        return done

    mine = slice(2 * PR, 3 * PR)
    late = lax.broadcasted_iota(jnp.int32, (PR, 32), 0) >= 2

    def run(at, wide, narrow):
        for step in range(1, RELAX):
            for c in range(2):
                for k in wide if step < 4 else narrow:
                    advance(step, c, k)
        for c in range(2):
            final = advance(RELAX, c, at + 2)
            for s in range(4):
                lanes = slice((s // 2) * 64 + 16, (s // 2) * 64 + 48)
                mesh_out[s, c] = final[s % 2][:PR, lanes]
                f = own_ref[c * PR : (c + 1) * PR, s * 32 : (s + 1) * 32]
                if s == 0:
                    f = jnp.where(late, flow[c, 0, at][mine, lanes], f)
                flow_out[s, c] = f

    @pl.when(sa == 0)
    def _():
        run(0, range(2, ns + 1), range(2, 4))

    @pl.when(sa != 0)
    def _():
        run(sa, range(2, ns + 2), [sa + 1, sa + 2, sa + 3])


PAIR = {0: 1, 1: 0, 2: 3, 3: 2}
CROSS = {1: 2, 2: 1}
RING = {1: 2, 2: 1, 0: 3, 3: 0}
SKIP = {0: 2, 2: 0, 1: 3, 3: 1}


def trade(array, axis, partner):
    sizes = [lax.axis_size(a) for a in AXES]
    route = []
    for x, y, k in np.ndindex(*sizes):
        place = {"gx": x, "chip": y // 2, "sa": k}
        target = (x, y ^ 1, k)
        if place[axis] in partner:
            place[axis] = partner[place[axis]]
            target = (place["gx"], place["chip"] * 2 + y % 2, place["sa"])
        route.append((
            int(np.ravel_multi_index((x, y, k), sizes)),
            int(np.ravel_multi_index(target, sizes)),
        ))
    return lax.ppermute(array, AXES, route)


def spread(load):
    near = trade(load, "gx", PAIR)
    far = trade(load, "gx", CROSS)
    odd = lax.axis_index("gx") % 2 == 1
    place = lax.broadcasted_iota(jnp.int32, load.shape, 1) % 64
    side = jnp.where((place < 16) == odd, near, far)
    load = jnp.where((place >= 16) & (place < 48), load, side)
    load = jnp.stack([load, trade(load, "gx", {})])
    near = trade(load, "chip", PAIR)
    far = trade(load, "chip", CROSS)
    load = jnp.stack([load, near, far])
    one = trade(load, "sa", PAIR)
    two = trade(load, "sa", RING)
    three = trade(load, "sa", SKIP)
    return jnp.stack([load, one, two, three])


def per_device(pixels, peak_offsets, validity):
    count, height, breadth = pixels.shape
    blocks = breadth // LANES
    size = lax.axis_size("sa")
    half = height // 2
    vmem = lambda: pl.BlockSpec(memory_space=pltpu.VMEM)
    held = pltpu.with_memory_space_constraint(pixels, pltpu.HBM)
    up, down, extra = pl.pallas_call(
        send_kernel,
        in_specs=[pl.BlockSpec(memory_space=pltpu.HBM)] * 2,
        out_specs=[vmem()] * 3,
        out_shape=[
            jax.ShapeDtypeStruct((half, breadth), BF),
            jax.ShapeDtypeStruct((half, breadth), BF),
            jax.ShapeDtypeStruct((8, 128), BF),
        ],
        scratch_shapes=[
            pltpu.VMEM((2, PR, 32), jnp.int32),
            pltpu.VMEM((8, 128), F32),
            pltpu.SemaphoreType.DMA((3,)),
        ],
        compiler_params=pltpu.CompilerParams(vmem_limit_bytes=GRANT),
        name="send",
    )(held, pltpu.with_memory_space_constraint(peak_offsets, pltpu.HBM))
    rise = [(i, (i + 1) % size) for i in range(size)]
    sink = [(i, (i - 1) % size) for i in range(size)]
    up = lax.ppermute(up, "sa", rise)
    down = lax.ppermute(down, "sa", sink)
    extra = lax.ppermute(extra, "sa", sink)

    rows = jnp.asarray(row_matrix())
    cols = jnp.asarray(col_matrix())
    second = jnp.asarray(second_matrix(blocks))
    whole = lambda shape: pl.BlockSpec(shape, lambda j: (0,) * len(shape))
    table_specs = [
        whole((2 * KROWS, PR * PATCH)),
        whole((256, 256)),
        whole((64, 2 * KROWS)),
        pl.BlockSpec((1, 2 * LANES, 8 * blocks * HELD), lambda j: (j, 0, 0)),
    ]
    inner, ready, mix = pl.pallas_call(
        inner_kernel,
        grid=(blocks,),
        in_specs=[pl.BlockSpec((count, height, LANES), lambda j: (0, 0, j))]
        + table_specs
        + [whole((count, 2, PR, 32)), whole((count, PR, 32))],
        out_specs=[
            whole((8, 128)),
            whole((24, 128)),
            pl.BlockSpec((2 * KROWS, LANES), lambda j: (0, j)),
        ],
        out_shape=[
            jax.ShapeDtypeStruct((8, 128), F32),
            jax.ShapeDtypeStruct((24, 128), F32),
            jax.ShapeDtypeStruct((2 * KROWS, breadth), BF),
        ],
        scratch_shapes=[
            pltpu.VMEM((96, 256), F32),
            pltpu.VMEM((SPAN, 12, 256), F32),
            pltpu.VMEM((2, 12, 32), jnp.int32),
        ],
        compiler_params=pltpu.CompilerParams(dimension_semantics=("arbitrary",), vmem_limit_bytes=GRANT),
        cost_estimate=pl.CostEstimate(
            flops=8 * 10**9, bytes_accessed=8 * 2**20, transcendentals=10**6
        ),
        name="inner",
    )(
        held, rows, cols, jnp.asarray(first_matrix(False)), second, peak_offsets, validity,
    )

    own, load = pl.pallas_call(
        edge_kernel,
        in_specs=[vmem()] * 11,
        out_specs=[vmem(), vmem()],
        out_shape=[
            jax.ShapeDtypeStruct((8, 128), F32),
            jax.ShapeDtypeStruct((24, 128), BF),
        ],
        scratch_shapes=[
            pltpu.VMEM((2, PR, 32), jnp.int32),
            pltpu.VMEM((24, 128), F32),
        ],
        compiler_params=pltpu.CompilerParams(vmem_limit_bytes=GRANT),
        name="edge",
    )(
        up, down, extra, mix, rows, cols, jnp.asarray(first_matrix(True)), second,
        inner, ready, peak_offsets,
    )

    got = spread(load)

    field = (count, 2, PR, 32)
    stack = (2, size, 24, 128)
    return pl.pallas_call(
        relax_kernel,
        in_specs=[vmem(), vmem()],
        out_specs=[vmem(), vmem()],
        out_shape=[jax.ShapeDtypeStruct(field, F32)] * 2,
        scratch_shapes=[
            pltpu.VMEM((3,) + stack, F32),
            pltpu.VMEM((2,) + stack, F32),
            pltpu.VMEM((5, 2, size + 4, 24, 128), F32),
            pltpu.VMEM((2, 2, 2, size + 4, 24, 128), F32),
        ],
        compiler_params=pltpu.CompilerParams(vmem_limit_bytes=GRANT),
        name="relax",
    )(got, own)


def solution(mesh):
    return jax.shard_map(
        per_device,
        mesh=mesh,
        in_specs=(P("sa", "gy", "gx"), P("sa", None, "gy", "gx"), P("sa", "gy", "gx")),
        out_specs=(P("sa", None, "gy", "gx"), P("sa", None, "gy", "gx")),
        check_vma=False,
    )
```

```python
import math

import jax
import jax.numpy as jnp
import numpy as np
from jax import lax
from jax.experimental import pallas as pl
from jax.experimental.pallas import tpu as pltpu
from jax.sharding import PartitionSpec as P


PATCH = 64
RELAX = 8
HALF = PATCH // 2 + 1
PR = 4
KROWS = 144
LANES = 512
SUB = LANES // 128
HELD = LANES // PATCH
REACH = 3
SPAN = 2 * REACH + 1
GRANT = 20 * 2**20
AXES = ("gx", "gy", "sa")

spring_plane = 0.5
spring_stack = 1.0
step_size = 0.2
damping = 0.6
whiten_floor = 1024.0

BF = jnp.bfloat16
F32 = jnp.float32


def wave_tables():
    angles = np.arange(PATCH, dtype=np.float32) * np.float32(2.0 * math.pi / PATCH)
    cosine = np.cos(angles).astype(BF).astype(np.float32)
    sine = np.sin(angles).astype(BF).astype(np.float32)
    return cosine, sine


def row_matrix():
    cosine, sine = wave_tables()
    out = np.zeros((2, KROWS, PR * PATCH), np.float32)
    phase = np.arange(HALF)[:, None] * np.arange(PATCH)[None, :] % PATCH
    for pr in range(PR):
        rows = slice(pr * HALF, (pr + 1) * HALF)
        cols = slice(pr * PATCH, (pr + 1) * PATCH)
        out[0, rows, cols] = cosine[phase]
        out[1, rows, cols] = -sine[phase]
    return out.reshape(2 * KROWS, PR * PATCH).astype(BF)


def col_matrix():
    cosine, sine = wave_tables()
    phase = np.arange(PATCH)[:, None] * np.arange(PATCH)[None, :] % PATCH
    out = np.zeros((2, 2, PATCH, 2, 2, PATCH), np.float32)
    for p in range(2):
        out[0, p, :, 0, p] = cosine[phase]
        out[1, p, :, 0, p] = sine[phase]
        out[0, p, :, 1, p] = -sine[phase]
        out[1, p, :, 1, p] = cosine[phase]
    return out.reshape(256, 256).astype(BF)


def first_matrix(flip):
    cosine, sine = wave_tables()
    out = np.zeros((2, 32, 2, KROWS), np.float32)
    k1 = np.arange(HALF)
    weight = np.where((k1 == 0) | (k1 == PATCH // 2), 1.0, 2.0)
    for p1 in range(SPAN):
        phase = k1 * (p1 - REACH) % PATCH
        for pr in range(PR):
            sign = -1.0 if flip and pr >= PR // 2 else 1.0
            row, cols = p1 * PR + pr, slice(pr * HALF, (pr + 1) * HALF)
            out[0, row, 0, cols] = weight * cosine[phase]
            out[0, row, 1, cols] = -sign * weight * sine[phase]
            out[1, row, 0, cols] = weight * sine[phase]
            out[1, row, 1, cols] = sign * weight * cosine[phase]
    return out.reshape(64, 2 * KROWS).astype(BF)


def second_matrix(blocks):
    cosine, sine = wave_tables()
    out = np.zeros((blocks, 2, HELD, PATCH, 8, blocks, HELD), np.float32)
    k2 = np.arange(PATCH)
    for p2 in range(SPAN):
        phase = k2 * (p2 - REACH) % PATCH
        for j in range(blocks):
            for p in range(HELD):
                out[j, 0, p, :, p2, j, p] = cosine[phase]
                out[j, 1, p, :, p2, j, p] = -sine[phase]
    return out.reshape(blocks, 2 * LANES, 8 * blocks * HELD).astype(BF)


def whiten(now, old):
    real, imag = [], []
    for (now_real, now_imag), (old_real, old_imag) in zip(now, old):
        cross_real = now_real * old_real + now_imag * old_imag
        cross_imag = now_imag * old_real - now_real * old_imag
        power = cross_real * cross_real + cross_imag * cross_imag
        inverse = lax.rsqrt(power + whiten_floor * whiten_floor)
        real.append((cross_real * inverse).astype(BF))
        imag.append((cross_imag * inverse).astype(BF))
    return jnp.concatenate(
        [jnp.concatenate(real, axis=1), jnp.concatenate(imag, axis=1)], axis=0
    )


def first_sum(table_ref, prod):
    both = jnp.dot(table_ref[...], prod, preferred_element_type=F32)
    return jnp.concatenate([both[:32], both[32:]], axis=1)


def send_kernel(px_ref, offs_ref, up_ref, down_ref, extra_ref, offs, low, sems):
    half = up_ref.shape[0]
    last = px_ref.shape[0] - 1
    copies = [
        pltpu.make_async_copy(offs_ref.at[0], offs, sems.at[0]),
        pltpu.make_async_copy(px_ref.at[last, pl.ds(0, half)], up_ref, sems.at[1]),
        pltpu.make_async_copy(px_ref.at[0, pl.ds(half, half)], down_ref, sems.at[2]),
    ]
    for copy in copies:
        copy.start()
    low[...] = jnp.zeros_like(low)
    copies[0].wait()
    for c in range(2):
        low[c * 2 : c * 2 + 2, :32] = offs[c, 2:4].astype(F32)
    extra_ref[...] = low[...].astype(BF)
    for copy in copies[1:]:
        copy.wait()


def row_sum(strips, rows_ref):
    return jnp.dot(rows_ref[...], strips, preferred_element_type=F32).astype(BF)


def col_sum(half, cols_ref):
    both = []
    for b in range(SUB):
        lanes = slice(b * 128, (b + 1) * 128)
        both.append(jnp.concatenate([half[:KROWS, lanes], half[KROWS:, lanes]], axis=1))
    spec = jnp.dot(jnp.concatenate(both, axis=0), cols_ref[...], preferred_element_type=F32)
    out = []
    for b in range(SUB):
        rows = slice(b * KROWS, (b + 1) * KROWS)
        out.append((spec[rows, :128], spec[rows, 128:]))
    return out


def pick(pieces, offset):
    value = pieces[0]
    for i in range(1, 5):
        value = jnp.where(offset == i - 2, pieces[i], value)
    return value


def peak_step(low, center, high):
    bend = jnp.maximum(jnp.abs(low - 2.0 * center + high), 1.0)
    return (low - high) / (2.0 * bend)


def refine(layers, row_off, col_off):
    wide = jnp.concatenate([row_off] * 8, axis=1)
    low, mid, high = [pick(layers[d : d + 5], wide) for d in range(3)]

    def cut(layer, d):
        return pick([layer[:, (d + i) * 32 : (d + i + 1) * 32] for i in range(5)], col_off)

    center = cut(mid, 1)
    return (
        row_off.astype(F32) + peak_step(cut(low, 1), center, cut(high, 1)),
        col_off.astype(F32) + peak_step(cut(mid, 0), center, cut(mid, 2)),
    )


def lay(ref, c, s, field):
    ring = jnp.concatenate([field[:, 16:], field, field[:, :16]], axis=1)
    at = (s % 2) * 12 + c * PR
    ref[at : at + PR, (s // 2) * 64 : (s // 2 + 1) * 64] = ring


def inner_kernel(
    px_ref, rows_ref, cols_ref, first_ref, second_ref, offs_ref, valid_ref,
    flow_ref, load_ref, mix_ref, corr_ref, picked, offs,
):
    count = px_ref.shape[0]
    sums, specs = [], []
    half = row_sum(px_ref[0], rows_ref)
    prod = None
    for s in range(count):
        specs.append(col_sum(half, cols_ref))
        if s + 1 < count:
            half = row_sum(px_ref[s + 1], rows_ref)
        if prod is not None:
            sums.append(first_sum(first_ref, prod).astype(BF))
        prod = whiten(specs[s], specs[s - 1]) if s else None
    sums.append(first_sum(first_ref, prod).astype(BF))
    edge, old = specs[0], specs[-1]
    low = lax.broadcasted_iota(jnp.int32, (KROWS, 128), 0) < 2 * HALF
    for b in range(SUB):
        for part in range(2):
            mix_ref[part * KROWS : (part + 1) * KROWS, b * 128 : (b + 1) * 128] = jnp.where(
                low, edge[b][part], old[b][part]
            ).astype(BF)
    term = jnp.dot(jnp.concatenate(sums, axis=0), second_ref[0], preferred_element_type=F32)

    @pl.when(pl.program_id(0) == 0)
    def _():
        corr_ref[...] = term

    @pl.when(pl.program_id(0) > 0)
    def _():
        corr_ref[...] += term

    @pl.when(pl.program_id(0) == pl.num_programs(0) - 1)
    def _():
        flow_ref[...] = jnp.zeros_like(flow_ref)
        load_ref[...] = jnp.zeros_like(load_ref)
        for s in range(1, count):
            rows = slice((s - 1) * PR, s * PR)
            for p1 in range(SPAN):
                at = (s - 1) * 32 + p1 * PR
                picked[p1, rows] = corr_ref[at : at + PR] * (1.0 / PATCH)
            for c in range(2):
                offs[c, rows] = offs_ref[s, c]
        flows = refine([picked[p1] for p1 in range(SPAN)], offs[0], offs[1])
        for s in range(count):
            lay(load_ref, 2, s, valid_ref[s].astype(F32))
            for c in range(2 if s else 0):
                piece = flows[c][(s - 1) * PR : s * PR]
                lay(load_ref, c, s, piece)
                flow_ref[c * PR : (c + 1) * PR, s * 32 : (s + 1) * 32] = piece


def edge_kernel(
    up_ref, down_ref, extra_ref, mix_ref, rows_ref, cols_ref, first_ref, second_ref,
    inner_ref, ready_ref, offs_ref, flow_ref, load_ref, offs, packed,
):
    sa = lax.axis_index("sa")
    breadth = mix_ref.shape[1]
    pr = lax.broadcasted_iota(jnp.int32, (32, 2 * LANES), 0) % PR
    dropped = ((sa == 0) & (pr < 2)) | ((sa == lax.axis_size("sa") - 1) & (pr >= 2))

    def strips(j):
        lanes = slice(j * LANES, (j + 1) * LANES)
        return jnp.concatenate([up_ref[:, lanes], down_ref[:, lanes]], axis=0)

    blocks = breadth // LANES
    corr = jnp.zeros((32, 256), F32)
    row = row_sum(strips(0), rows_ref)
    prod = None
    for j in range(blocks + 1):
        if j < blocks:
            there = col_sum(row, cols_ref)
            if j + 1 < blocks:
                row = row_sum(strips(j + 1), rows_ref)
        if j:
            sums = first_sum(first_ref, prod)
            sums = jnp.where(dropped, 0.0, sums).astype(BF)
            corr += jnp.dot(sums, second_ref[j - 1], preferred_element_type=F32)
        if j < blocks:
            here = []
            for b in range(SUB * j, SUB * (j + 1)):
                part = slice(b * 128, (b + 1) * 128)
                here.append((mix_ref[:KROWS, part].astype(F32), mix_ref[KROWS:, part].astype(F32)))
            prod = whiten(here, there)

    extra = extra_ref[...].astype(F32).astype(jnp.int32)
    for c in range(2):
        offs[c] = offs_ref[0, c]
        offs[c, 2:4, :] = extra[c * 2 : c * 2 + 2, :32]
    layers = [corr[p1 * PR : (p1 + 1) * PR] * (1.0 / PATCH) for p1 in range(SPAN)]
    flows = refine(layers, offs[0], offs[1])
    flow_ref[...] = inner_ref[...]
    packed[...] = ready_ref[...]
    for c in range(2):
        flow_ref[c * PR : (c + 1) * PR, :32] = flows[c]
        lay(packed, c, 0, flows[c])
    load_ref[...] = packed[...].astype(BF)


def relax_kernel(got_ref, own_ref, flow_out, mesh_out, raw, flow, coef, state):
    gx, gy, sa = [lax.axis_index(a) for a in AXES]
    nx, ny, ns = [lax.axis_size(a) for a in AXES]
    shape = (24, 128)
    lane = lax.broadcasted_iota(jnp.int32, shape, 1)
    row = lax.broadcasted_iota(jnp.int32, shape, 0)
    low = lane < 64
    for c in range(3):
        for i in range(2):
            for k in range(ns):
                raw[c, i, k, 20:, :] = jnp.zeros((4, 128), F32)
    for g in range(5):
        chip = (gy + g) // 2 - gy // 2 - 1
        pair = (chip < 0) == (gy // 2 % 2 == 1)
        chip = jnp.where(chip == 0, 0, jnp.where(pair, 1, 2))
        core = g % 2
        for k in range(ns):
            hop = sa ^ k
            block = got_ref[hop ^ (hop // 2), core, chip].astype(F32)
            for i in range(2):
                for c in range(3):
                    raw[c, i, k, g * PR : (g + 1) * PR, :] = block[
                        i * 12 + c * PR : i * 12 + (c + 1) * PR
                    ]

    place = gy * PR - 2 * PR + row
    column = gx * 32 - 16 + lane % 64
    ok = (place >= 0) & (place < ny * PR) & (row < 5 * PR) & (column >= 0) & (column < nx * 32)
    inside = jnp.where(ok, 1.0, 0.0)
    edges = jnp.where(place == 0, 1.0, 0.0) + jnp.where(place == ny * PR - 1, 1.0, 0.0)
    edges += jnp.where(column == 0, 1.0, 0.0) + jnp.where(column == nx * 32 - 1, 1.0, 0.0)
    degree = 4.0 - edges
    zero = jnp.zeros(shape, F32)

    blank = (0, 1, ns + 2, ns + 3)
    for k in blank:
        for i in range(2):
            for c in range(2):
                state[0, c, i, k] = zero
                state[1, c, i, k] = zero
            if k in (1, ns + 2):
                for c in range(5):
                    coef[c, i, k] = zero

    swapped = (row % PR >= 2) & low
    for c in range(2):
        carry = zero
        for k in range(ns):
            even = jnp.where(swapped, raw[c, 0, (k + ns - 1) % ns], raw[c, 0, k]) * inside
            odd = raw[c, 1, k] * inside
            flow[c, 0, k] = even
            flow[c, 1, k] = odd
            pair = even + odd
            turned = pltpu.roll(pair, 64, 1)
            even = even + jnp.where(low, 0.0, turned) + carry
            odd = even + odd
            for old in range(2):
                state[old, c, 0, k + 2] = even
                state[old, c, 1, k + 2] = odd
            carry = carry + pair + turned

    def turn(array):
        return pltpu.roll(array, 64, 1)

    plane = inside * (step_size * spring_plane)
    stack = inside * (step_size * spring_stack)
    for k in range(ns):
        weights = [raw[2, i, k] * stack for i in range(2)]
        later = raw[2, 0, k + 1] * stack if k + 1 < ns else 0.0
        nexts = [weights[1], turn(jnp.where(low, later, weights[0]))]
        for i in range(2):
            coef[0, i, k + 2] = weights[i]
            coef[1, i, k + 2] = nexts[i]
            coef[2, i, k + 2] = 1.0 + damping - degree * plane - weights[i] - nexts[i]
        for c in range(2):
            later = flow[c, 0, k + 1] if k + 1 < ns else 0.0
            ahead = [flow[c, 1, k], turn(jnp.where(low, later, flow[c, 0, k]))]
            for i in range(2):
                coef[3 + c, i, k + 2] = weights[i] * flow[c, i, k] - nexts[i] * ahead[i]

    def advance(step, c, k):
        src, dst = (step + 1) % 2, step % 2
        top = 8 if step == RELAX else 0
        end = 24 if step < 4 else 16
        rows, read = slice(top, end), slice(0, end)
        now = [state[src, c, i, k, read] for i in range(2)]
        here = [m[rows] for m in now]
        edge = low[rows]
        behind = [
            turn(jnp.where(edge, here[1], state[src, c, 1, k - 1, rows])),
            here[0],
        ]
        ahead = [
            here[1],
            turn(jnp.where(edge, state[src, c, 0, k + 1, rows], here[0])),
        ]
        done = []
        for i in range(2):
            around = pltpu.roll(here[i], 1, 1) + pltpu.roll(here[i], 127, 1)
            around += pltpu.roll(now[i], 1, 0)[rows]
            if step == 4:
                around += pltpu.roll(state[src, c, i, k], 23, 0)[rows]
            else:
                around += pltpu.roll(now[i], end - 1, 0)[rows]
            m = coef[2, i, k, rows] * here[i] - damping * state[dst, c, i, k, rows]
            m += plane[rows] * around + coef[3 + c, i, k, rows]
            m += coef[0, i, k, rows] * behind[i] + coef[1, i, k, rows] * ahead[i]
            if step < RELAX:
                state[dst, c, i, k, rows] = m
            done.append(m)
        return done

    mine = slice(2 * PR, 3 * PR)
    late = lax.broadcasted_iota(jnp.int32, (PR, 32), 0) >= 2

    def run(at, wide, narrow):
        for step in range(1, RELAX):
            for c in range(2):
                for k in wide if step < 4 else narrow:
                    advance(step, c, k)
        for c in range(2):
            final = advance(RELAX, c, at + 2)
            for s in range(4):
                lanes = slice((s // 2) * 64 + 16, (s // 2) * 64 + 48)
                mesh_out[s, c] = final[s % 2][:PR, lanes]
                f = own_ref[c * PR : (c + 1) * PR, s * 32 : (s + 1) * 32]
                if s == 0:
                    f = jnp.where(late, flow[c, 0, at][mine, lanes], f)
                flow_out[s, c] = f

    @pl.when(sa == 0)
    def _():
        run(0, range(2, ns + 1), range(2, 4))

    @pl.when(sa != 0)
    def _():
        run(sa, range(2, ns + 2), [sa + 1, sa + 2, sa + 3])


PAIR = {0: 1, 1: 0, 2: 3, 3: 2}
CROSS = {1: 2, 2: 1}
RING = {1: 2, 2: 1, 0: 3, 3: 0}
SKIP = {0: 2, 2: 0, 1: 3, 3: 1}


def trade(array, axis, partner):
    sizes = [lax.axis_size(a) for a in AXES]
    route = []
    for x, y, k in np.ndindex(*sizes):
        place = {"gx": x, "chip": y // 2, "sa": k}
        target = (x, y ^ 1, k)
        if place[axis] in partner:
            place[axis] = partner[place[axis]]
            target = (place["gx"], place["chip"] * 2 + y % 2, place["sa"])
        route.append((
            int(np.ravel_multi_index((x, y, k), sizes)),
            int(np.ravel_multi_index(target, sizes)),
        ))
    return lax.ppermute(array, AXES, route)


def spread(load):
    near = trade(load, "gx", PAIR)
    far = trade(load, "gx", CROSS)
    odd = lax.axis_index("gx") % 2 == 1
    place = lax.broadcasted_iota(jnp.int32, load.shape, 1) % 64
    side = jnp.where((place < 16) == odd, near, far)
    load = jnp.where((place >= 16) & (place < 48), load, side)
    near = trade(load, "chip", PAIR)
    far = trade(load, "chip", CROSS)
    load = jnp.stack([load, near, far])
    load = jnp.stack([load, trade(load, "gx", {})])
    one = trade(load, "sa", PAIR)
    two = trade(load, "sa", RING)
    three = trade(load, "sa", SKIP)
    return jnp.stack([load, one, two, three])


def per_device(pixels, peak_offsets, validity):
    count, height, breadth = pixels.shape
    blocks = breadth // LANES
    size = lax.axis_size("sa")
    half = height // 2
    vmem = lambda: pl.BlockSpec(memory_space=pltpu.VMEM)
    held = pltpu.with_memory_space_constraint(pixels, pltpu.HBM)
    up, down, extra = pl.pallas_call(
        send_kernel,
        in_specs=[pl.BlockSpec(memory_space=pltpu.HBM)] * 2,
        out_specs=[vmem()] * 3,
        out_shape=[
            jax.ShapeDtypeStruct((half, breadth), BF),
            jax.ShapeDtypeStruct((half, breadth), BF),
            jax.ShapeDtypeStruct((8, 128), BF),
        ],
        scratch_shapes=[
            pltpu.VMEM((2, PR, 32), jnp.int32),
            pltpu.VMEM((8, 128), F32),
            pltpu.SemaphoreType.DMA((3,)),
        ],
        compiler_params=pltpu.CompilerParams(vmem_limit_bytes=GRANT),
        name="send",
    )(held, pltpu.with_memory_space_constraint(peak_offsets, pltpu.HBM))
    rise = [(i, (i + 1) % size) for i in range(size)]
    sink = [(i, (i - 1) % size) for i in range(size)]
    up = lax.ppermute(up, "sa", rise)
    down = lax.ppermute(down, "sa", sink)
    extra = lax.ppermute(extra, "sa", sink)

    rows = jnp.asarray(row_matrix())
    cols = jnp.asarray(col_matrix())
    second = jnp.asarray(second_matrix(blocks))
    whole = lambda shape: pl.BlockSpec(shape, lambda j: (0,) * len(shape))
    table_specs = [
        whole((2 * KROWS, PR * PATCH)),
        whole((256, 256)),
        whole((64, 2 * KROWS)),
        pl.BlockSpec((1, 2 * LANES, 8 * blocks * HELD), lambda j: (j, 0, 0)),
    ]
    inner, ready, mix = pl.pallas_call(
        inner_kernel,
        grid=(blocks,),
        in_specs=[pl.BlockSpec((count, height, LANES), lambda j: (0, 0, j))]
        + table_specs
        + [whole((count, 2, PR, 32)), whole((count, PR, 32))],
        out_specs=[
            whole((8, 128)),
            whole((24, 128)),
            pl.BlockSpec((2 * KROWS, LANES), lambda j: (0, j)),
        ],
        out_shape=[
            jax.ShapeDtypeStruct((8, 128), F32),
            jax.ShapeDtypeStruct((24, 128), F32),
            jax.ShapeDtypeStruct((2 * KROWS, breadth), BF),
        ],
        scratch_shapes=[
            pltpu.VMEM((96, 256), F32),
            pltpu.VMEM((SPAN, 12, 256), F32),
            pltpu.VMEM((2, 12, 32), jnp.int32),
        ],
        compiler_params=pltpu.CompilerParams(dimension_semantics=("arbitrary",), vmem_limit_bytes=GRANT),
        cost_estimate=pl.CostEstimate(
            flops=8 * 10**9, bytes_accessed=8 * 2**20, transcendentals=10**6
        ),
        name="inner",
    )(
        held,
        *[
            pltpu.with_memory_space_constraint(table, pltpu.HBM)
            for table in (
                rows, cols, jnp.asarray(first_matrix(False)), second, peak_offsets, validity,
            )
        ],
    )

    own, load = pl.pallas_call(
        edge_kernel,
        in_specs=[vmem()] * 11,
        out_specs=[vmem(), vmem()],
        out_shape=[
            jax.ShapeDtypeStruct((8, 128), F32),
            jax.ShapeDtypeStruct((24, 128), BF),
        ],
        scratch_shapes=[
            pltpu.VMEM((2, PR, 32), jnp.int32),
            pltpu.VMEM((24, 128), F32),
        ],
        compiler_params=pltpu.CompilerParams(vmem_limit_bytes=GRANT),
        name="edge",
    )(
        up, down, extra, mix, rows, cols, jnp.asarray(first_matrix(True)), second,
        inner, ready, peak_offsets,
    )

    got = spread(load)

    field = (count, 2, PR, 32)
    stack = (2, size, 24, 128)
    return pl.pallas_call(
        relax_kernel,
        in_specs=[vmem(), vmem()],
        out_specs=[vmem(), vmem()],
        out_shape=[jax.ShapeDtypeStruct(field, F32)] * 2,
        scratch_shapes=[
            pltpu.VMEM((3,) + stack, F32),
            pltpu.VMEM((2,) + stack, F32),
            pltpu.VMEM((5, 2, size + 4, 24, 128), F32),
            pltpu.VMEM((2, 2, 2, size + 4, 24, 128), F32),
        ],
        compiler_params=pltpu.CompilerParams(vmem_limit_bytes=GRANT),
        name="relax",
    )(got, own)


def solution(mesh):
    return jax.shard_map(
        per_device,
        mesh=mesh,
        in_specs=(P("sa", "gy", "gx"), P("sa", None, "gy", "gx"), P("sa", "gy", "gx")),
        out_specs=(P("sa", None, "gy", "gx"), P("sa", None, "gy", "gx")),
        check_vma=False,
    )
```
